256 devices in a mesh: ctx: 16 (over y, x_lo, core), hs: 16 (over x_hi, z).
Axes of the slice: x: 4 (x_hi: 2, x_lo: 2; x = x_hi * 2 + x_lo), y: 4, z: 8, core: 2. Of those that a mesh axis runs over, the one named last changes fastest.
Arguments:
- queries: bfloat16 [16, 16384, 512], P('hs', 'ctx'), may hold values from -40 to 40
- keys: bfloat16 [16, 16384, 512], P('hs', 'ctx'), may hold values from -6 to 6
- values: bfloat16 [16, 16384, 512], P('hs', 'ctx'), may hold values from -6 to 6
- rates: float32 [16, 16384], P('hs', 'ctx'), may hold values from 0.02 to 0.2
- doc_ids: int32 [2, 16384], replicated, may hold values from 0 to 3, never falling along the last dimension, each value on 1 to 8192 neighbouring positions
- fast_weights: bfloat16 [16, 3, 512, 512], P('hs'), may hold values from -0.25 to 0.25
- momentum: float32 [16, 3, 512, 512], P('hs'), may hold values from -0.2 to 0.2
- head_gain: float32 [16, 512], P('hs'), may hold values from 0.5 to 2
Outputs:
- tokens_out: bfloat16 [16, 16384, 512], P('hs', 'ctx')
- new_weights: bfloat16 [16, 3, 512, 512], P('hs')
The draws below stay inside these ranges and needn't reach their ends.
Inputs may be any that keep to these rules, and one draw needn't show every extreme that they name: `doc_ids`: each row never falls; a document has at most 8192 positions and some document has exactly that many.
All inputs are finite; a program needn't handle non-finite values.
Results may differ from the reference program's by a relative error of at most 0.0092.
Values may be sent and summed in bfloat16 or wider, within the bound.
No kernel may reach another device: no remote copies, remote signals or barrier semaphores. Data moves between devices by JAX's collectives and lax.ppermute only.
A program may use at most 64 MiB of HBM per device.

```python
import math
import jax
import jax.numpy as jnp
import numpy as np
from jax import lax

DH = 512
FH = 512
WINDOW_TOKENS = 512
SEQS = 2
TOKENS = 16384
PAIRS = 16
HEADS = 8


def joint_draw(key):
    base = jax.random.fold_in(key, 911)
    first, second = jax.random.split(base, 2)
    shape = (PAIRS, TOKENS, DH)
    keyset = jnp.clip(jax.random.normal(first, shape, jnp.float32), -4.0, 4.0)
    queryset = jnp.clip(jax.random.normal(second, shape, jnp.float32), -4.0, 4.0)
    return (queryset, keyset)


def draw_queries(key, part):
    return joint_draw(key)[0].astype(jnp.bfloat16)


def draw_keys(key, part):
    return joint_draw(key)[1].astype(jnp.bfloat16)


def block_scale(stream_key, dims, shards, low, top_value):
    def one(position, shards_of):
        draws = jax.random.uniform(jax.random.fold_in(jax.random.fold_in(stream_key, 6), position), (shards_of,), jnp.float32, low / len(shards), top_value / len(shards))
        return jnp.repeat(jnp.exp(draws), dims[position] // shards_of).reshape((-1,) + (1,) * (len(dims) - position - 1))

    loudness = one(*shards[0])
    for cut in shards[1:]:
        loudness = loudness * one(*cut)
    return loudness


def profile(number_of, total, reach, skew):
    portions = [(1 << 20) // math.isqrt(grade ** skew) + 1 for grade in range(2, number_of + 1)]
    rest, holding = total - reach - (number_of - 1), [1] * (number_of - 1)
    while rest > 0:
        candidates = [i for i in range(number_of - 1) if holding[i] < reach]
        mass, budget = sum([portions[i] for i in candidates]), rest
        for i in candidates:
            extra = min(reach - holding[i], max(1, budget * portions[i] // mass), rest)
            holding[i] = holding[i] + extra
            rest = rest - extra
    return np.array([reach] + holding)


def ragged_sizes(rng, number_of, total, limit, lean):
    if number_of == 2:
        one = jax.random.randint(rng, (), max(1, total - limit), min(limit, total - 1) + 1)
        return jnp.stack([one, total - one])
    tallies = jnp.asarray(profile(number_of, total, limit, lean), jnp.int32)
    pairs = (number_of - 1) // 2
    donor, receiver = tallies[1:1 + 2 * pairs:2], tallies[2:2 + 2 * pairs:2]
    margin = jnp.minimum(donor - 1, limit - receiver)
    shifted = jax.random.randint(jax.random.fold_in(rng, 1), (pairs,), 0, 1 << 20) % (margin + 1)
    tallies = tallies.at[1:1 + 2 * pairs:2].set(donor - shifted).at[2:2 + 2 * pairs:2].set(receiver + shifted)
    return tallies[jax.random.permutation(jax.random.fold_in(rng, 2), number_of)]


def bell_draw(key, shape, spread, reach, shards=(), held_as=jnp.bfloat16):
    level = block_scale(key, shape, shards, -0.22, 0.18) if shards else 1.0
    values = jax.random.normal(key, shape, jnp.float32) * spread * level
    return jnp.minimum(jnp.maximum(values, -reach), reach).astype(held_as)


def setup_inputs(seed: int = 0) -> dict:
    seeds = jax.random.split(jax.random.key(seed), 9)
    queries = draw_queries(jax.random.fold_in(seeds[8], 71), 0)
    keys = draw_keys(jax.random.fold_in(seeds[8], 71), 0)
    values = bell_draw(seeds[2], (PAIRS, TOKENS, DH), 1.0, 6.0, ((0, 16), (1, 16)))
    rates = jnp.clip(jnp.exp(math.log(0.2) - 2.3025851 * jax.random.uniform(seeds[3], (PAIRS, TOKENS), jnp.float32) ** block_scale(seeds[3], (PAIRS, TOKENS), ((0, 16), (1, 16)), -0.2, 0.2)), 0.02, 0.2)
    doc_ids = jax.vmap(lambda own: jnp.searchsorted(jnp.cumsum(ragged_sizes(own, 4, TOKENS, TOKENS // 2, 1)), jnp.arange(TOKENS), side="right"))(jax.random.split(seeds[4], SEQS)).reshape((SEQS, TOKENS)).astype(jnp.int32)
    fast_weights = bell_draw(seeds[5], (PAIRS, 3, DH, FH), DH ** -0.5, 0.25, ((0, 16),))
    momentum = bell_draw(seeds[6], (PAIRS, 3, DH, FH), 0.03, 0.2, ((0, 16),), jnp.float32)
    head_gain = jnp.clip(jnp.exp(math.log(2.0) - 1.3862944 * jax.random.uniform(seeds[7], (PAIRS, DH), jnp.float32) ** block_scale(seeds[7], (PAIRS, DH), ((0, 16),), -0.2, 0.2)), 0.5, 2.0)
    return dict(queries=queries, keys=keys, values=values, rates=rates, doc_ids=doc_ids, fast_weights=fast_weights, momentum=momentum, head_gain=head_gain)


def attend_block(qb, kb, value_block, qpos, kpos, qdoc, kdoc):
    scores = jnp.einsum('qd,kd->qk', qb, kb, preferred_element_type=jnp.float32) / math.sqrt(qb.shape[1])
    valid = (kpos[None, :] <= qpos[:, None]) & (kpos[None, :] > qpos[:, None] - WINDOW_TOKENS) & (kpos[None, :] >= 0) & (kdoc[None, :] == qdoc[:, None])
    scores = jnp.where(valid, scores, -1e+30)
    top = lax.optimization_barrier(jnp.max(scores, axis=1, keepdims=True))
    expo = jnp.where(valid, jnp.exp(scores - top), 0.0)
    probs = (expo / lax.optimization_barrier(jnp.sum(expo, axis=1, keepdims=True))).astype(jnp.bfloat16)
    return jnp.dot(probs, value_block, preferred_element_type=jnp.float32)

def renew(weights, mom_old, grads):
    mom = 0.9 * mom_old + grads
    wf = weights.astype(jnp.float32)
    cand = wf - mom
    old_rms = jnp.sqrt(lax.optimization_barrier(jnp.mean(wf * wf, axis=1, keepdims=True)) + 1e-06)
    new_rms = jnp.sqrt(lax.optimization_barrier(jnp.mean(cand * cand, axis=1, keepdims=True)) + 1e-06)
    return (cand * old_rms / new_rms).astype(jnp.bfloat16)

def one_pair(packed):
    qrow, krow, value_row_index, lrow, weights, mom_old, docrow = packed
    zeroed_rows = jnp.zeros((WINDOW_TOKENS, DH), jnp.bfloat16)
    kpad = jnp.concatenate([zeroed_rows, krow], axis=0)
    value_padded = jnp.concatenate([zeroed_rows, value_row_index], axis=0)
    dpad = jnp.concatenate([jnp.zeros((WINDOW_TOKENS,), jnp.int32), docrow], axis=0)

    def block(index):
        begin_offset = (index * WINDOW_TOKENS).astype(jnp.int32)
        qb = lax.dynamic_slice_in_dim(qrow, begin_offset, WINDOW_TOKENS, 0)
        kb = lax.dynamic_slice_in_dim(kpad, begin_offset, 2 * WINDOW_TOKENS, 0)
        value_block = lax.dynamic_slice_in_dim(value_padded, begin_offset, 2 * WINDOW_TOKENS, 0)
        qpos = begin_offset + jnp.arange(WINDOW_TOKENS, dtype=jnp.int32)
        kpos = begin_offset - WINDOW_TOKENS + jnp.arange(2 * WINDOW_TOKENS, dtype=jnp.int32)
        qdoc = lax.dynamic_slice_in_dim(docrow, begin_offset, WINDOW_TOKENS, 0)
        kdoc = lax.dynamic_slice_in_dim(dpad, begin_offset, 2 * WINDOW_TOKENS, 0)
        return attend_block(qb, kb, value_block, qpos, kpos, qdoc, kdoc)
    attn = lax.map(block, jnp.arange(TOKENS // WINDOW_TOKENS, dtype=jnp.int32)).reshape(TOKENS, DH)
    h1 = jnp.dot(krow, weights[0], preferred_element_type=jnp.float32)
    h3 = jnp.dot(krow, weights[1], preferred_element_type=jnp.float32)
    act = jax.nn.silu(h1)
    gk = (act * h3).astype(jnp.bfloat16)
    scaled = (lrow[:, None] * value_row_index.astype(jnp.float32) / math.sqrt(TOKENS)).astype(jnp.bfloat16)
    dg = -jnp.dot(scaled, weights[2], preferred_element_type=jnp.float32)
    sig = jax.nn.sigmoid(h1)
    dh1 = (dg * h3 * sig * (1.0 + h1 * (1.0 - sig))).astype(jnp.bfloat16)
    dh3 = (dg * act).astype(jnp.bfloat16)
    g_one = jnp.einsum('td,tf->df', krow, dh1, preferred_element_type=jnp.float32)
    g_three = jnp.einsum('td,tf->df', krow, dh3, preferred_element_type=jnp.float32)
    g_down = -jnp.einsum('td,tf->df', scaled, gk, preferred_element_type=jnp.float32)
    grads = jnp.stack([g_one, g_three, g_down])
    fresh = renew(weights, mom_old, grads)
    o_one = jnp.dot(qrow, fresh[0], preferred_element_type=jnp.float32)
    o_three = jnp.dot(qrow, fresh[1], preferred_element_type=jnp.float32)
    gq = (jax.nn.silu(o_one) * o_three).astype(jnp.bfloat16)
    fast_out = jnp.einsum('tf,df->td', gq, fresh[2], preferred_element_type=jnp.float32)
    return (attn + fast_out, fresh)

def reference(queries, keys, values, rates, doc_ids, fast_weights, momentum, head_gain):
    pair_seq = (jnp.arange(PAIRS, dtype=jnp.int32) // HEADS).astype(jnp.int32)
    docrows = doc_ids[pair_seq]
    mixed, fresh = lax.map(one_pair, (queries, keys, values, rates, fast_weights, momentum, docrows))
    squares = lax.optimization_barrier(jnp.sum(mixed * mixed, axis=2)).reshape(SEQS, HEADS, TOKENS)
    totals = lax.optimization_barrier(jnp.sum(squares, axis=1))
    scale_rows = 1.0 / jnp.sqrt(totals / (HEADS * DH) + 1e-06)

    def normalize(packed):
        yrow, gain, seq = packed
        srow = lax.dynamic_index_in_dim(scale_rows, seq, 0, keepdims=False)
        return (yrow * srow[:, None] * gain[None, :]).astype(jnp.bfloat16)
    tokens_out = lax.map(normalize, (mixed, head_gain, pair_seq))
    return (tokens_out, fresh)
```

```python
import functools
import math

import jax
import jax.numpy as jnp
from jax import lax
from jax.experimental import pallas as pl
from jax.experimental.pallas import tpu as pltpu
from jax.sharding import Mesh, PartitionSpec as P

WINDOW = 512
TILE = 256
BLOCK = 16
MIB = 1024 * 1024
BF16 = jnp.bfloat16
F32 = jnp.float32
NEG = -1e30

Y, X, CORE, SEQ, HEAD = "y", "x", "core", "seq", "head"


def nt(a, b):
    return lax.dot_general(a, b, (((1,), (1,)), ((), ())), preferred_element_type=F32)


def nn(a, b):
    return lax.dot_general(a, b, (((1,), (0,)), ((), ())), preferred_element_type=F32)


def tn(a, b):
    return lax.dot_general(a, b, (((0,), (0,)), ((), ())), preferred_element_type=F32)


def whole():
    return pl.BlockSpec(memory_space=pltpu.VMEM)


def params(limit, **kw):
    return pltpu.CompilerParams(vmem_limit_bytes=limit * MIB, **kw)


def cost(flops, read, trans=0):
    return pl.CostEstimate(flops=int(flops), bytes_accessed=int(read), transcendentals=int(trans))


def column_of(row):
    return jnp.transpose(jnp.broadcast_to(row, (128, 128)))


def grad_kernel(inv, me_ref, k_ref, v_ref, r_ref, w_ref, keep_ref, send_ref, acc):
    step = pl.program_id(0)

    @pl.when(step == 0)
    def _():
        acc[...] = jnp.zeros_like(acc)

    keys = k_ref[0]
    tiles = TILE // 128
    parts = []
    for t in range(tiles):
        rate = column_of(r_ref[pl.ds(step * tiles + t, 1), :])
        rows = v_ref[0, t * 128 : (t + 1) * 128, :].astype(F32)
        wide = jnp.concatenate([rate] * (rows.shape[1] // 128), axis=1)
        parts.append((wide * rows * inv).astype(BF16))
    u = jnp.concatenate(parts, axis=0)
    h1 = nn(keys, w_ref[0, 0])
    h3 = nn(keys, w_ref[0, 1])
    dg = nn(u, w_ref[0, 2])
    sig = 0.5 + 0.5 * jnp.tanh(0.5 * h1)
    act = h1 * sig
    gk = (act * h3).astype(BF16)
    dh3 = (dg * act).astype(BF16)
    dh1 = (dg * h3 * (sig + act * (1.0 - sig))).astype(BF16)
    acc[0] += tn(dh1, keys)
    acc[1] += tn(dh3, keys)
    acc[2] += tn(gk, u)

    @pl.when(step == pl.num_programs(0) - 1)
    def _():
        me = me_ref[0]
        half = keep_ref.shape[0]
        for l in range(2 * half):
            at = pl.multiple_of((me ^ l) * BLOCK, BLOCK)
            rows = acc[:, pl.ds(at, BLOCK), :].astype(BF16)
            if l < half:
                keep_ref[l] = rows
            else:
                send_ref[l - half] = rows


def grad_half(half, me, keys, values, rates, weights, inv):
    rows, dim = keys.shape[1:]
    hidden = weights.shape[3] // 2
    blocks = hidden // BLOCK // 2
    out = jax.ShapeDtypeStruct((blocks, 3, BLOCK, dim), BF16)
    return pl.pallas_call(
        functools.partial(grad_kernel, inv),
        grid_spec=pltpu.PrefetchScalarGridSpec(
            num_scalar_prefetch=1,
            grid=(rows // TILE,),
            in_specs=[
                pl.BlockSpec((1, TILE, dim), lambda i, s: (0, i, 0)),
                pl.BlockSpec((1, TILE, dim), lambda i, s: (0, i, 0)),
                pl.BlockSpec(rates.shape, lambda i, s: (0, 0)),
                pl.BlockSpec((1, 3, dim, hidden), lambda i, s: (0, 0, 0, half)),
            ],
            out_specs=[pl.BlockSpec(out.shape, lambda i, s: (0, 0, 0, 0))] * 2,
            scratch_shapes=[pltpu.VMEM((3, hidden, dim), F32)],
        ),
        out_shape=[out, out],
        compiler_params=params(20),
        cost_estimate=cost(12 * rows * dim * hidden, 4 * MIB, rows * hidden),
        name="grad" + "ab"[half],
    )(me, keys, values, rates, weights)


def attend(q, ks, vs, first, low, scale):
    tile = q.shape[0]
    col = lax.broadcasted_iota(jnp.int32, (tile, tile), 1)
    row = lax.broadcasted_iota(jnp.int32, (tile, tile), 0)
    scores = []
    for b in range(3):
        s = nt(q, ks[b])
        ok = col >= low - (first + b * tile)
        if b == 2:
            ok = ok & (col <= row)
        scores.append(jnp.where(ok, s, NEG))
    top = jnp.max(jnp.maximum(jnp.maximum(scores[0], scores[1]), scores[2]), axis=1, keepdims=True)
    total, out = None, None
    for b in range(3):
        p = jnp.exp2((scores[b] - top) * scale)
        total = p if total is None else total + p
        o = nn(p.astype(BF16), vs[b])
        out = o if out is None else out + o
    return out / jnp.sum(total, axis=1, keepdims=True)


def lowest(meta_ref, first, tile):
    pos = first + 2 * tile + lax.broadcasted_iota(jnp.int32, (tile, 1), 0)
    low = jnp.zeros_like(pos)
    for b in range(1, 4):
        low = jnp.where(pos >= meta_ref[b], meta_ref[b], low)
    return jnp.maximum(low, pos - (WINDOW - 1))


def attn_kernel(scale, part, meta_ref, *refs):
    if part == 0:
        q_ref, rk_ref, rv_ref, k_ref, v_ref, o_ref = refs
    else:
        q_ref, k_ref, v_ref, o_ref = refs
    for t in range(WINDOW // TILE):
        first = meta_ref[0] + part * WINDOW + (t - 2) * TILE
        ks, vs = [], []
        for b in range(3):
            at = part * WINDOW + (t + b - 2) * TILE
            if at < 0:
                at += WINDOW
                ks.append(rk_ref[at : at + TILE, :])
                vs.append(rv_ref[at : at + TILE, :])
            else:
                ks.append(k_ref[0, at : at + TILE, :])
                vs.append(v_ref[0, at : at + TILE, :])
        q = q_ref[0, t * TILE : (t + 1) * TILE, :]
        o_ref[t * TILE : (t + 1) * TILE, :] = attend(
            q, ks, vs, first, lowest(meta_ref, first, TILE), scale
        )


def attention(part, meta, queries, rims, keys, values):
    dim = queries.shape[2]
    rows = keys.shape[1] if part else WINDOW
    smem = pl.BlockSpec(memory_space=pltpu.SMEM)
    own = pl.BlockSpec((1, rows, dim), lambda i: (0, 0, 0))
    rim = pl.BlockSpec((WINDOW, dim), lambda i: (0, 0))
    return pl.pallas_call(
        functools.partial(attn_kernel, math.log2(math.e) / math.sqrt(dim), part),
        grid=(1,),
        in_specs=[smem, pl.BlockSpec((1, WINDOW, dim), lambda i: (0, part, 0))]
        + [rim] * len(rims)
        + [own, own],
        out_specs=pl.BlockSpec((WINDOW, dim), lambda i: (0, 0)),
        out_shape=jax.ShapeDtypeStruct((WINDOW, dim), F32),
        compiler_params=params(20),
        cost_estimate=cost(4 * WINDOW * 3 * TILE * dim, 4 * MIB, 3 * WINDOW * TILE),
        name="attn" + "ab"[part],
    )(meta, queries, *rims, keys, values)


def prep_kernel(me_ref, w_ref, m_ref, base_ref, rms_ref, wt, mt):
    half = pl.program_id(0)
    me = jnp.where(half == 0, me_ref[0], me_ref[1])
    at = pl.multiple_of((me % 8) * BLOCK, BLOCK)
    for m in range(3):
        wt[...] = jnp.transpose(w_ref[0, m].astype(F32))
        mt[...] = jnp.transpose(m_ref[0, m])
        w = wt[pl.ds(at, BLOCK), :]
        base_ref[0, m] = w - 0.9 * mt[pl.ds(at, BLOCK), :]
        rms = jnp.sqrt(jnp.mean(w * w, axis=1, keepdims=True) + 1e-06)
        rms_ref[0, m] = jnp.broadcast_to(rms, (BLOCK, 128))


def prepare(me, weights, momentum):
    dim, hidden = weights.shape[2:]
    pick = lambda i, s: (0, 0, 0, 2 * i + jnp.where(i == 0, s[0], s[1]) // 8)
    return pl.pallas_call(
        prep_kernel,
        grid_spec=pltpu.PrefetchScalarGridSpec(
            num_scalar_prefetch=1,
            grid=(2,),
            in_specs=[pl.BlockSpec((1, 3, dim, 128), pick)] * 2,
            out_specs=[
                pl.BlockSpec((1, 3, BLOCK, dim), lambda i, s: (i, 0, 0, 0)),
                pl.BlockSpec((1, 3, BLOCK, 128), lambda i, s: (i, 0, 0, 0)),
            ],
            scratch_shapes=[pltpu.VMEM((128, dim), F32)] * 2,
        ),
        out_shape=[
            jax.ShapeDtypeStruct((2, 3, BLOCK, dim), F32),
            jax.ShapeDtypeStruct((2, 3, BLOCK, 128), F32),
        ],
        compiler_params=params(12),
        cost_estimate=cost(3 * MIB, 3 * MIB),
        name="prep",
    )(me, weights, momentum)


def renew_kernel(half, base_ref, rms_ref, *refs):
    out_ref = refs[-1]
    neg = refs[0][...].astype(F32).reshape(out_ref.shape)
    for r in refs[1:-1]:
        neg = neg + r[...].astype(F32).reshape(out_ref.shape)
    cand = base_ref[half] + neg
    new = lax.rsqrt(jnp.mean(cand * cand, axis=2, keepdims=True) + 1e-06)
    out_ref[...] = (cand * (rms_ref[half][:, :, :1] * new)).astype(BF16)


def renew(half, base, rms, pieces):
    return pl.pallas_call(
        functools.partial(renew_kernel, half),
        in_specs=[whole()] * (2 + len(pieces)),
        out_specs=whole(),
        out_shape=jax.ShapeDtypeStruct(base.shape[1:], BF16),
        compiler_params=params(8),
        cost_estimate=cost(MIB, MIB // 2),
        name="renew" + "ab"[half],
    )(base, rms, *pieces)


def fill(new, mine_ref, other_ref):
    half, _, block, dim = mine_ref.shape
    for m in range(3):
        new[m, : half * block, :] = mine_ref[:, m].reshape(half * block, dim)
        new[m, half * block :, :] = other_ref[:, m].reshape(half * block, dim)


def fast_part(q, new):
    one = nt(q, new[0])
    three = nt(q, new[1])
    gq = (one * (0.5 + 0.5 * jnp.tanh(0.5 * one)) * three).astype(BF16)
    return nn(gq, new[2])


def out_a_kernel(q_ref, lo_ref, hi_ref, mine_ref, other_ref, y_ref, new):
    step = pl.program_id(0)

    @pl.when(step == 0)
    def _():
        fill(new, mine_ref, other_ref)

    attn = jnp.where(step < pl.num_programs(0) // 2, lo_ref[...], hi_ref[...])
    y_ref[...] = attn + fast_part(q_ref[0], new)


def out_b_kernel(q_ref, y1_ref, mine_ref, other_ref, y_ref, ss_ref, new):
    step = pl.program_id(0)

    @pl.when(step == 0)
    def _():
        fill(new, mine_ref, other_ref)

    y = y1_ref[...] + fast_part(q_ref[0], new)
    y_ref[...] = y
    sq = y * y
    lanes = sq[:, :128]
    for c in range(1, sq.shape[1] // 128):
        lanes = lanes + sq[:, c * 128 : (c + 1) * 128]
    tiles = TILE // 128
    for t in range(tiles):
        turned = jnp.transpose(lanes[t * 128 : (t + 1) * 128, :])
        ss_ref[pl.ds(step * tiles + t, 1), :] = jnp.sum(turned, axis=0, keepdims=True)


def out_a(queries, lo, hi, mine, other):
    rows, dim = queries.shape[1:]
    hidden = 2 * mine.shape[0] * BLOCK
    half = rows // TILE // 2
    full = pl.BlockSpec(mine.shape, lambda i: (0, 0, 0, 0))
    return pl.pallas_call(
        out_a_kernel,
        grid=(rows // TILE,),
        in_specs=[
            pl.BlockSpec((1, TILE, dim), lambda i: (0, i, 0)),
            pl.BlockSpec((TILE, dim), lambda i: (jnp.minimum(i, half - 1), 0)),
            pl.BlockSpec((TILE, dim), lambda i: (jnp.maximum(i - half, 0), 0)),
            full,
            full,
        ],
        out_specs=pl.BlockSpec((TILE, dim), lambda i: (i, 0)),
        out_shape=jax.ShapeDtypeStruct((rows, dim), F32),
        scratch_shapes=[pltpu.VMEM((3, hidden, dim), BF16)],
        compiler_params=params(16),
        cost_estimate=cost(6 * rows * dim * hidden, 6 * MIB, rows * hidden),
        name="outa",
    )(queries, lo, hi, mine, other)


def out_b(queries, y1, mine, other):
    rows, dim = queries.shape[1:]
    hidden = 2 * mine.shape[0] * BLOCK
    full = pl.BlockSpec(mine.shape, lambda i: (0, 0, 0, 0))
    return pl.pallas_call(
        out_b_kernel,
        grid=(rows // TILE,),
        in_specs=[
            pl.BlockSpec((1, TILE, dim), lambda i: (0, i, 0)),
            pl.BlockSpec((TILE, dim), lambda i: (i, 0)),
            full,
            full,
        ],
        out_specs=[
            pl.BlockSpec((TILE, dim), lambda i: (i, 0)),
            pl.BlockSpec((rows // 128, 128), lambda i: (0, 0)),
        ],
        out_shape=[
            jax.ShapeDtypeStruct((rows, dim), F32),
            jax.ShapeDtypeStruct((rows // 128, 128), F32),
        ],
        scratch_shapes=[pltpu.VMEM((3, hidden, dim), BF16)],
        compiler_params=params(16),
        cost_estimate=cost(6 * rows * dim * hidden, 6 * MIB, rows * hidden),
        name="outb",
    )(queries, y1, mine, other)


def weights_kernel(me_ref, am_ref, ao_ref, bm_ref, bo_ref, out_ref, rows):
    half = am_ref.shape[0]
    for m in range(3):
        for h, (mine, other) in enumerate(((am_ref, ao_ref), (bm_ref, bo_ref))):
            for l in range(2 * half):
                at = pl.multiple_of(((me_ref[h] ^ l) + h * 2 * half) * BLOCK, BLOCK)
                rows[pl.ds(at, BLOCK), :] = mine[l, m] if l < half else other[l - half, m]
        out_ref[0, m] = jnp.transpose(rows[...])


def weights_out(me, am, ao, bm, bo):
    dim = am.shape[3]
    hidden = 4 * am.shape[0] * BLOCK
    return pl.pallas_call(
        weights_kernel,
        in_specs=[pl.BlockSpec(memory_space=pltpu.SMEM)] + [whole()] * 4,
        out_specs=whole(),
        out_shape=jax.ShapeDtypeStruct((1, 3, dim, hidden), BF16),
        scratch_shapes=[pltpu.VMEM((hidden, dim), BF16)],
        compiler_params=params(12),
        cost_estimate=cost(MIB, 3 * MIB),
        name="weightsout",
    )(me, am, ao, bm, bo)


def norm_kernel(count, y_ref, a_ref, b_ref, gain_ref, out_ref):
    step = pl.program_id(0)
    tiles = y_ref.shape[0] // 128
    dim = y_ref.shape[1]
    gain = gain_ref[...]
    for t in range(tiles):
        at = pl.ds(step * tiles + t, 1)
        total = a_ref[at, :] + b_ref[at, :]
        scale = column_of(lax.rsqrt(total * (1.0 / count) + 1e-06))
        wide = jnp.concatenate([scale] * (dim // 128), axis=1)
        rows = slice(t * 128, (t + 1) * 128)
        out_ref[0, rows, :] = (y_ref[rows, :] * wide * gain).astype(BF16)


def norm(y, a, b, gain, count):
    rows, dim = y.shape
    small = pl.BlockSpec(a.shape, lambda i: (0, 0))
    return pl.pallas_call(
        functools.partial(norm_kernel, count),
        grid=(rows // TILE,),
        in_specs=[
            pl.BlockSpec((TILE, dim), lambda i: (i, 0)),
            small,
            small,
            pl.BlockSpec((1, dim), lambda i: (0, 0)),
        ],
        out_specs=pl.BlockSpec((1, TILE, dim), lambda i: (0, i, 0)),
        out_shape=jax.ShapeDtypeStruct((1, rows, dim), BF16),
        compiler_params=params(12),
        cost_estimate=cost(MIB, 3 * MIB),
        name="norm",
    )(y, a, b, gain)


def swap(x, axis, by):
    return lax.ppermute(x, axis, [(i, i ^ by) for i in range(lax.axis_size(axis))])


def added(*xs):
    return sum(x.astype(F32) for x in xs).astype(BF16)


def scatter_a(keep, send):
    got = swap(send, CORE, 1)
    n = keep.shape[0] // 2
    keep, send = added(keep[:n], got[:n]), added(keep[n:], got[n:])
    got = swap(send, X, 1)
    s = [added(keep[k : k + 1], got[k : k + 1]) for k in range(keep.shape[0])]
    return [s[0]] + [swap(s[k], Y, k) for k in range(1, len(s))]


def scatter_b(keep, send):
    got = swap(send, CORE, 1)
    s = [added(keep[2 * k : 2 * k + 2], got[2 * k : 2 * k + 2]) for k in range(keep.shape[0] // 2)]
    got = [swap(s[k], Y, k) for k in range(1, len(s))]
    keep = added(s[0][:1], *(g[:1] for g in got))
    send = added(s[0][1:], *(g[1:] for g in got))
    return [keep, swap(send, X, 1)]


def gather_a(new):
    new = new[None]
    new = jnp.concatenate([new] + [swap(new, Y, k) for k in range(1, lax.axis_size(Y))], axis=0)
    new = jnp.concatenate([new, swap(new, X, 1)], axis=0)
    return new, swap(new, CORE, 1)


def gather_b(new):
    new = new[None]
    new = jnp.concatenate([new, swap(new, X, 1)], axis=0)
    new = jnp.concatenate([new] + [swap(new, Y, k) for k in range(1, lax.axis_size(Y))], axis=0)
    return new, swap(new, CORE, 1)


def ring_sum(s):
    n = lax.axis_size(HEAD)
    s = s + swap(s, HEAD, 1)
    s = s + lax.ppermute(s, HEAD, [(i, (i + 1) % n if i % 2 else (i - 1) % n) for i in range(n)])
    far = lax.ppermute(s, HEAD, [((d - 3) % n if d % 2 else (d + 3) % n, d) for d in range(n)])
    return s, far


def per_device(queries, keys, values, rates, doc_ids, fast_weights, momentum, head_gain):
    rows, dim = queries.shape[1:]
    ys, xs, cores = lax.axis_size(Y), lax.axis_size(X), lax.axis_size(CORE)
    y, x, core = lax.axis_index(Y), lax.axis_index(X), lax.axis_index(CORE)
    ctx = (Y, X, CORE)
    n = ys * xs * cores
    me_a = (core * xs + x) * ys + y
    me_b = (core * ys + y) * xs + x
    me = jnp.stack([me_a, me_b]).astype(jnp.int32)
    offset = lax.axis_index(ctx) * rows
    docs = lax.dynamic_index_in_dim(doc_ids, lax.axis_index(SEQ), 0, keepdims=False)
    bounds = jnp.sum(
        docs[None, :] < jnp.arange(1, 4, dtype=jnp.int32)[:, None], axis=1, dtype=jnp.int32
    )
    meta = jnp.concatenate([offset.astype(jnp.int32)[None], bounds])
    ahead = [(i, i + 1) for i in range(n - 1)]
    rim_keys = lax.ppermute(keys[0, rows - WINDOW :], ctx, ahead)
    rim_values = lax.ppermute(values[0, rows - WINDOW :], ctx, ahead)
    rate_rows = rates.reshape(rows // 128, 128)
    inv = 1.0 / math.sqrt(rows * n)

    part_a = grad_half(0, me[0:1], keys, values, rate_rows, fast_weights, inv)
    part_b = grad_half(1, me[1:2], keys, values, rate_rows, fast_weights, inv)
    base, rms = prepare(me, fast_weights, momentum)
    pieces_a = scatter_a(*part_a)
    pieces_b = scatter_b(*part_b)
    hi = attention(1, meta, queries, (), keys, values)
    lo = attention(0, meta, queries, (rim_keys, rim_values), keys, values)
    new_a = renew(0, base, rms, pieces_a)
    new_b = renew(1, base, rms, pieces_b)
    full_a = gather_a(new_a)
    full_b = gather_b(new_b)
    mixed = out_a(queries, lo, hi, *full_a)
    mixed, squares = out_b(queries, mixed, *full_b)
    sums = ring_sum(squares)
    fresh = weights_out(me, *full_a, *full_b)
    result = norm(mixed, *sums, head_gain, lax.axis_size(HEAD) * dim)
    return result, fresh


def solution(mesh):
    seqs = 2
    sizes = mesh.shape
    fine = Mesh(
        mesh.devices.reshape(sizes["ctx"] // 4, 2, 2, seqs, sizes["hs"] // seqs),
        (Y, X, CORE, SEQ, HEAD),
    )
    ctx, hs = (Y, X, CORE), (SEQ, HEAD)
    return jax.shard_map(
        per_device,
        mesh=fine,
        in_specs=(
            P(hs, ctx, None),
            P(hs, ctx, None),
            P(hs, ctx, None),
            P(hs, ctx),
            P(),
            P(hs, None, None, None),
            P(hs, None, None, None),
            P(hs, None),
        ),
        out_specs=(P(hs, ctx, None), P(hs, None, None, None)),
        check_vma=False,
    )
```

```python
import functools
import math

import jax
import jax.numpy as jnp
from jax import lax
from jax.experimental import pallas as pl
from jax.experimental.pallas import tpu as pltpu
from jax.sharding import Mesh, PartitionSpec as P

WINDOW = 512
TILE = 256
BLOCK = 16
MIB = 1024 * 1024
BF16 = jnp.bfloat16
F32 = jnp.float32
NEG = -1e30

Y, X, CORE, SEQ, HEAD = "y", "x", "core", "seq", "head"


def nt(a, b):
    return lax.dot_general(a, b, (((1,), (1,)), ((), ())), preferred_element_type=F32)


def nn(a, b):
    return lax.dot_general(a, b, (((1,), (0,)), ((), ())), preferred_element_type=F32)


def tn(a, b):
    return lax.dot_general(a, b, (((0,), (0,)), ((), ())), preferred_element_type=F32)


def whole():
    return pl.BlockSpec(memory_space=pltpu.VMEM)


def params(limit, **kw):
    return pltpu.CompilerParams(vmem_limit_bytes=limit * MIB, **kw)


def cost(flops, read, trans=0):
    return pl.CostEstimate(flops=int(flops), bytes_accessed=int(read), transcendentals=int(trans))


def column_of(row):
    return jnp.transpose(jnp.broadcast_to(row, (128, 128)))


def grad_kernel(inv, me_ref, k_ref, v_ref, r_ref, w_ref, keep_ref, send_ref, kk, uu, dd, acc):
    step = pl.program_id(0)
    last = pl.num_programs(0) - 1
    here = pl.ds(pl.multiple_of(step * TILE, TILE), TILE)
    keys = k_ref[0]
    kk[here, :] = keys
    tiles = TILE // 128
    parts = []
    for t in range(tiles):
        rate = column_of(r_ref[0:1, t * 128 : (t + 1) * 128])
        rows = v_ref[0, t * 128 : (t + 1) * 128, :].astype(F32)
        wide = jnp.concatenate([rate] * (rows.shape[1] // 128), axis=1)
        parts.append((wide * rows * inv).astype(BF16))
    u = jnp.concatenate(parts, axis=0)
    uu[here, :] = u
    h1 = nn(keys, w_ref[0, 0])
    h3 = nn(keys, w_ref[0, 1])
    dg = nn(u, w_ref[0, 2])
    sig = 0.5 + 0.5 * jnp.tanh(0.5 * h1)
    act = h1 * sig
    dd[0, here, :] = (dg * h3 * (sig + act * (1.0 - sig))).astype(BF16)
    dd[1, here, :] = (dg * act).astype(BF16)
    dd[2, here, :] = (act * h3).astype(BF16)

    @pl.when(step == last)
    def _():
        acc[0] = tn(dd[0], kk[...]).astype(BF16)
        acc[1] = tn(dd[1], kk[...]).astype(BF16)
        acc[2] = tn(dd[2], uu[...]).astype(BF16)
        half = keep_ref.shape[1]
        for h in range(2):
            me = me_ref[h]
            for l in range(2 * half):
                at = pl.multiple_of(((me ^ l) + h * 2 * half) * BLOCK, BLOCK)
                rows = acc[:, pl.ds(at, BLOCK), :]
                if l < half:
                    keep_ref[h, l] = rows
                else:
                    send_ref[h, l - half] = rows


def gradients(me, keys, values, rates, weights, inv):
    rows, dim = keys.shape[1:]
    hidden = weights.shape[3]
    blocks = hidden // BLOCK // 4
    out = jax.ShapeDtypeStruct((2, blocks, 3, BLOCK, dim), BF16)
    tile = pl.BlockSpec((1, TILE, dim), lambda i, s: (0, i, 0))
    return pl.pallas_call(
        functools.partial(grad_kernel, inv),
        grid_spec=pltpu.PrefetchScalarGridSpec(
            num_scalar_prefetch=1,
            grid=(rows // TILE,),
            in_specs=[
                tile,
                tile,
                pl.BlockSpec((1, TILE), lambda i, s: (0, i)),
                pl.BlockSpec(weights.shape, lambda i, s: (0, 0, 0, 0)),
            ],
            out_specs=[whole()] * 2,
            scratch_shapes=[
                pltpu.VMEM((rows, dim), BF16),
                pltpu.VMEM((rows, dim), BF16),
                pltpu.VMEM((3, rows, hidden), BF16),
                pltpu.VMEM((3, hidden, dim), BF16),
            ],
        ),
        out_shape=[out, out],
        compiler_params=params(24),
        cost_estimate=cost(12 * rows * dim * hidden, 6 * MIB, rows * hidden),
        name="grad",
    )(me, keys, values, rates, weights)


def rim_kernel(k_ref, v_ref, rim_ref):
    rim_ref[0] = k_ref[0]
    rim_ref[1] = v_ref[0]


def rim_of(keys, values):
    rows, dim = keys.shape[1:]
    end = pl.BlockSpec((1, WINDOW, dim), lambda i: (0, rows // WINDOW - 1, 0))
    return pl.pallas_call(
        rim_kernel,
        grid=(1,),
        in_specs=[end, end],
        out_specs=whole(),
        out_shape=jax.ShapeDtypeStruct((2, WINDOW, dim), BF16),
        compiler_params=params(6),
        cost_estimate=cost(1, 3 * MIB),
        name="rim",
    )(keys, values)


def attend(q, ks, vs, first, low, scale):
    tile = q.shape[0]
    col = lax.broadcasted_iota(jnp.int32, (tile, tile), 1)
    row = lax.broadcasted_iota(jnp.int32, (tile, tile), 0)
    scores = []
    for b in range(3):
        s = nt(q, ks[b])
        ok = col >= low - (first + b * tile)
        if b == 2:
            ok = ok & (col <= row)
        scores.append(jnp.where(ok, s, NEG))
    top = jnp.max(jnp.maximum(jnp.maximum(scores[0], scores[1]), scores[2]), axis=1, keepdims=True)
    total, out = None, None
    for b in range(3):
        p = jnp.exp2((scores[b] - top) * scale)
        total = p if total is None else total + p
        o = nn(p.astype(BF16), vs[b])
        out = o if out is None else out + o
    return out / jnp.sum(total, axis=1, keepdims=True)


def lowest(meta_ref, first, tile):
    pos = first + 2 * tile + lax.broadcasted_iota(jnp.int32, (tile, 1), 0)
    low = jnp.zeros_like(pos)
    for b in range(1, 4):
        low = jnp.where(pos >= meta_ref[b], meta_ref[b], low)
    return jnp.maximum(low, pos - (WINDOW - 1))


def attn_kernel(scale, part, meta_ref, *refs):
    if part == 0:
        q_ref, rim_ref, k_ref, v_ref, o_ref = refs
    else:
        q_ref, k_ref, v_ref, o_ref = refs
    for t in range(WINDOW // TILE):
        first = meta_ref[0] + part * WINDOW + (t - 2) * TILE
        ks, vs = [], []
        for b in range(3):
            at = part * WINDOW + (t + b - 2) * TILE
            if at < 0:
                at += WINDOW
                ks.append(rim_ref[0, at : at + TILE, :])
                vs.append(rim_ref[1, at : at + TILE, :])
            else:
                ks.append(k_ref[0, at : at + TILE, :])
                vs.append(v_ref[0, at : at + TILE, :])
        q = q_ref[0, t * TILE : (t + 1) * TILE, :]
        o_ref[t * TILE : (t + 1) * TILE, :] = attend(
            q, ks, vs, first, lowest(meta_ref, first, TILE), scale
        )


def attention(part, meta, queries, rims, keys, values):
    dim = queries.shape[2]
    rows = keys.shape[1] if part else WINDOW
    smem = pl.BlockSpec(memory_space=pltpu.SMEM)
    own = pl.BlockSpec((1, rows, dim), lambda i: (0, 0, 0))
    rim = pl.BlockSpec((2, WINDOW, dim), lambda i: (0, 0, 0))
    return pl.pallas_call(
        functools.partial(attn_kernel, math.log2(math.e) / math.sqrt(dim), part),
        grid=(1,),
        in_specs=[smem, pl.BlockSpec((1, WINDOW, dim), lambda i: (0, part, 0))]
        + [rim] * len(rims)
        + [own, own],
        out_specs=pl.BlockSpec((WINDOW, dim), lambda i: (0, 0)),
        out_shape=jax.ShapeDtypeStruct((WINDOW, dim), F32),
        compiler_params=params(14),
        cost_estimate=cost(4 * WINDOW * 3 * TILE * dim, 4 * MIB, 3 * WINDOW * TILE),
        name="attn" + "ab"[part],
    )(meta, queries, *rims, keys, values)


def prep_kernel(me_ref, w_ref, m_ref, base_ref, rms_ref, wt, mt):
    half = pl.program_id(0)
    me = jnp.where(half == 0, me_ref[0], me_ref[1])
    at = pl.multiple_of((me % 8) * BLOCK, BLOCK)
    for m in range(3):
        wt[...] = jnp.transpose(w_ref[0, m].astype(F32))
        mt[...] = jnp.transpose(m_ref[0, m])
        w = wt[pl.ds(at, BLOCK), :]
        base_ref[0, m] = w - 0.9 * mt[pl.ds(at, BLOCK), :]
        rms = jnp.sqrt(jnp.mean(w * w, axis=1, keepdims=True) + 1e-06)
        rms_ref[0, m] = jnp.broadcast_to(rms, (BLOCK, 128))


def prepare(me, weights, momentum):
    dim, hidden = weights.shape[2:]
    pick = lambda i, s: (0, 0, 0, 2 * i + jnp.where(i == 0, s[0], s[1]) // 8)
    return pl.pallas_call(
        prep_kernel,
        grid_spec=pltpu.PrefetchScalarGridSpec(
            num_scalar_prefetch=1,
            grid=(2,),
            in_specs=[pl.BlockSpec((1, 3, dim, 128), pick)] * 2,
            out_specs=[
                pl.BlockSpec((1, 3, BLOCK, dim), lambda i, s: (i, 0, 0, 0)),
                pl.BlockSpec((1, 3, BLOCK, 128), lambda i, s: (i, 0, 0, 0)),
            ],
            scratch_shapes=[pltpu.VMEM((128, dim), F32)] * 2,
        ),
        out_shape=[
            jax.ShapeDtypeStruct((2, 3, BLOCK, dim), F32),
            jax.ShapeDtypeStruct((2, 3, BLOCK, 128), F32),
        ],
        compiler_params=params(12),
        cost_estimate=cost(3 * MIB, 3 * MIB),
        name="prep",
    )(me, weights, momentum)


def renew_kernel(base_ref, rms_ref, a_ref, ga_ref, b_ref, gb_ref, *outs):
    for h, (one, two) in enumerate(((a_ref, ga_ref), (b_ref, gb_ref))):
        cand = base_ref[h] + (one[0].astype(F32) + two[0].astype(F32))
        new = lax.rsqrt(jnp.mean(cand * cand, axis=2, keepdims=True) + 1e-06)
        outs[h][0] = (cand * (rms_ref[h][:, :, :1] * new)).astype(BF16)


def renew(base, rms, *pieces):
    return pl.pallas_call(
        renew_kernel,
        in_specs=[whole()] * 6,
        out_specs=[whole()] * 2,
        out_shape=[jax.ShapeDtypeStruct((1,) + base.shape[1:], BF16)] * 2,
        compiler_params=params(8),
        cost_estimate=cost(MIB, MIB // 2),
        name="renew",
    )(base, rms, *pieces)


def fill(new, mine_ref, other_ref):
    _, half, _, block, dim = mine_ref.shape
    size = half * block
    for m in range(3):
        for h in range(2):
            new[m, 2 * h * size : (2 * h + 1) * size, :] = mine_ref[h, :, m].reshape(size, dim)
            new[m, (2 * h + 1) * size : (2 * h + 2) * size, :] = other_ref[h, :, m].reshape(size, dim)


def fast_part(q, new):
    one = nt(q, new[0])
    three = nt(q, new[1])
    gq = (one * (0.5 + 0.5 * jnp.tanh(0.5 * one)) * three).astype(BF16)
    return nn(gq, new[2])


def out_kernel(q_ref, lo_ref, hi_ref, mine_ref, other_ref, y_ref, ss_ref, new):
    step = pl.program_id(0)

    @pl.when(step == 0)
    def _():
        fill(new, mine_ref, other_ref)

    attn = jnp.where(step < pl.num_programs(0) // 2, lo_ref[...], hi_ref[...])
    y = attn + fast_part(q_ref[0], new)
    y_ref[...] = y
    sq = y * y
    lanes = sq[:, :128]
    for c in range(1, sq.shape[1] // 128):
        lanes = lanes + sq[:, c * 128 : (c + 1) * 128]
    tiles = TILE // 128
    for t in range(tiles):
        turned = jnp.transpose(lanes[t * 128 : (t + 1) * 128, :])
        ss_ref[pl.ds(step * tiles + t, 1), :] = jnp.sum(turned, axis=0, keepdims=True)


def outputs(queries, lo, hi, mine, other):
    rows, dim = queries.shape[1:]
    hidden = 4 * mine.shape[1] * BLOCK
    half = rows // TILE // 2
    full = pl.BlockSpec(mine.shape, lambda i: (0, 0, 0, 0, 0))
    return pl.pallas_call(
        out_kernel,
        grid=(rows // TILE,),
        in_specs=[
            pl.BlockSpec((1, TILE, dim), lambda i: (0, i, 0)),
            pl.BlockSpec((TILE, dim), lambda i: (jnp.minimum(i, half - 1), 0)),
            pl.BlockSpec((TILE, dim), lambda i: (jnp.maximum(i - half, 0), 0)),
            full,
            full,
        ],
        out_specs=[
            pl.BlockSpec((TILE, dim), lambda i: (i, 0)),
            pl.BlockSpec((rows // 128, 128), lambda i: (0, 0)),
        ],
        out_shape=[
            jax.ShapeDtypeStruct((rows, dim), F32),
            jax.ShapeDtypeStruct((rows // 128, 128), F32),
        ],
        scratch_shapes=[pltpu.VMEM((3, hidden, dim), BF16)],
        compiler_params=params(14),
        cost_estimate=cost(6 * rows * dim * hidden, 6 * MIB, rows * hidden),
        name="out",
    )(queries, lo, hi, mine, other)


def weights_kernel(me_ref, mine_ref, other_ref, out_ref, rows):
    half = mine_ref.shape[1]
    for m in range(3):
        for h in range(2):
            for l in range(2 * half):
                at = pl.multiple_of(((me_ref[h] ^ l) + h * 2 * half) * BLOCK, BLOCK)
                rows[pl.ds(at, BLOCK), :] = (
                    mine_ref[h, l, m] if l < half else other_ref[h, l - half, m]
                )
        out_ref[0, m] = jnp.transpose(rows[...])


def weights_out(me, mine, other):
    dim = mine.shape[4]
    hidden = 4 * mine.shape[1] * BLOCK
    return pl.pallas_call(
        weights_kernel,
        in_specs=[pl.BlockSpec(memory_space=pltpu.SMEM)] + [whole()] * 2,
        out_specs=whole(),
        out_shape=jax.ShapeDtypeStruct((1, 3, dim, hidden), BF16),
        scratch_shapes=[pltpu.VMEM((hidden, dim), BF16)],
        compiler_params=params(12),
        cost_estimate=cost(MIB, 3 * MIB),
        name="weightsout",
    )(me, mine, other)


def norm_kernel(count, y_ref, a_ref, b_ref, gain_ref, out_ref):
    step = pl.program_id(0)
    tiles = y_ref.shape[0] // 128
    dim = y_ref.shape[1]
    gain = gain_ref[...]
    for t in range(tiles):
        at = pl.ds(step * tiles + t, 1)
        total = a_ref[at, :] + b_ref[at, :]
        scale = column_of(lax.rsqrt(total * (1.0 / count) + 1e-06))
        wide = jnp.concatenate([scale] * (dim // 128), axis=1)
        rows = slice(t * 128, (t + 1) * 128)
        out_ref[0, rows, :] = (y_ref[rows, :] * wide * gain).astype(BF16)


def norm(y, a, b, gain, count):
    rows, dim = y.shape
    small = pl.BlockSpec(a.shape, lambda i: (0, 0))
    return pl.pallas_call(
        functools.partial(norm_kernel, count),
        grid=(rows // TILE,),
        in_specs=[
            pl.BlockSpec((TILE, dim), lambda i: (i, 0)),
            small,
            small,
            pl.BlockSpec((1, dim), lambda i: (0, 0)),
        ],
        out_specs=pl.BlockSpec((1, TILE, dim), lambda i: (0, i, 0)),
        out_shape=jax.ShapeDtypeStruct((1, rows, dim), BF16),
        compiler_params=params(12),
        cost_estimate=cost(MIB, 3 * MIB),
        name="norm",
    )(y, a, b, gain)


def swap(x, axis, by):
    return lax.ppermute(x, axis, [(i, i ^ by) for i in range(lax.axis_size(axis))])


def added_kernel(*refs):
    pairs = len(refs) // 4
    for p in range(pairs):
        keep, got = refs[2 * p], refs[2 * p + 1]
        n = keep.shape[0] // 2
        for o, part in ((0, slice(0, n)), (1, slice(n, 2 * n))):
            refs[2 * pairs + 2 * p + o][...] = (
                keep[part].astype(F32) + got[part].astype(F32)
            ).astype(BF16)


def first_kernel(keep_ref, got_ref, *outs):
    n = keep_ref.shape[1] // 2
    for h in range(2):
        for o, part in ((0, slice(0, n)), (1, slice(n, 2 * n))):
            outs[2 * h + o][...] = (
                keep_ref[h, part].astype(F32) + got_ref[h, part].astype(F32)
            ).astype(BF16)


def added(kernel, name, *arrays):
    n = arrays[0].shape[-4] // 2
    shape = (n,) + arrays[0].shape[-3:]
    return pl.pallas_call(
        kernel,
        in_specs=[whole()] * len(arrays),
        out_specs=[whole()] * 4,
        out_shape=[jax.ShapeDtypeStruct(shape, BF16)] * 4,
        compiler_params=params(8),
        cost_estimate=cost(MIB, MIB),
        name=name,
    )(*arrays)


def joined_kernel(a_ref, ga_ref, b_ref, gb_ref, *outs):
    n = a_ref.shape[0]
    for h, (one, two) in enumerate(((a_ref, ga_ref), (b_ref, gb_ref))):
        out = outs[h] if len(outs) == 2 else outs[0].at[h]
        out[:n] = one[...]
        out[n:] = two[...]


def joined(last, *arrays):
    n = arrays[0].shape[0]
    shape = (2 * n,) + arrays[0].shape[1:]
    outs = [jax.ShapeDtypeStruct((2,) + shape, BF16)] if last else [jax.ShapeDtypeStruct(shape, BF16)] * 2
    return pl.pallas_call(
        joined_kernel,
        in_specs=[whole()] * 4,
        out_specs=[whole()] * len(outs),
        out_shape=outs,
        compiler_params=params(8),
        cost_estimate=cost(1, MIB),
        name="join%d" % n,
    )(*arrays)


def ring_sum(s):
    n = lax.axis_size(HEAD)
    s = s + swap(s, HEAD, 1)
    s = s + lax.ppermute(s, HEAD, [(i, (i + 1) % n if i % 2 else (i - 1) % n) for i in range(n)])
    far = lax.ppermute(s, HEAD, [((d - 3) % n if d % 2 else (d + 3) % n, d) for d in range(n)])
    return s, far


def per_device(queries, keys, values, rates, doc_ids, fast_weights, momentum, head_gain):
    rows, dim = queries.shape[1:]
    y, x, core = lax.axis_index(Y), lax.axis_index(X), lax.axis_index(CORE)
    ctx = (Y, X, CORE)
    n = lax.axis_size(Y) * lax.axis_size(X) * lax.axis_size(CORE)
    far = y // 2
    near = (y + far) % 2
    me_a = core * 8 + x * 4 + near * 2 + far
    me_b = core * 8 + near * 4 + far * 2 + x
    me = jnp.stack([me_a, me_b]).astype(jnp.int32)
    offset = lax.axis_index(ctx) * rows
    docs = lax.dynamic_index_in_dim(doc_ids, lax.axis_index(SEQ), 0, keepdims=False)
    bounds = jnp.sum(
        docs[None, :] < jnp.arange(1, 4, dtype=jnp.int32)[:, None], axis=1, dtype=jnp.int32
    )
    meta = jnp.concatenate([offset.astype(jnp.int32)[None], bounds])
    inv = 1.0 / math.sqrt(rows * n)
    hbm = lambda array: pltpu.with_memory_space_constraint(array, pltpu.HBM)

    rim = rim_of(hbm(keys), hbm(values))
    rim, me = lax.optimization_barrier((rim, me))
    rim = lax.ppermute(rim, ctx, [(i, (i + 1) % n) for i in range(n)])
    keep, send = gradients(me, hbm(keys), hbm(values), rates, hbm(fast_weights), inv)
    got = swap(send, CORE, 1)
    ka, sa, kb, sb = added(first_kernel, "add8", keep, got)
    ga, gb = swap(sa, X, 1), swap(sb, Y, 1)
    ka, kb, meta = lax.optimization_barrier((ka, kb, meta))
    hi = attention(1, meta, queries, (), keys, values)
    ga, gb, hi = lax.optimization_barrier((ga, gb, hi))
    ka, sa, kb, sb = added(added_kernel, "add4", ka, ga, kb, gb)
    ga, gb = swap(sa, Y, 1), swap(sb, Y, 3)
    ka, kb, me = lax.optimization_barrier((ka, kb, me))
    base, rms = prepare(me, fast_weights, momentum)
    ga, gb, base, rms = lax.optimization_barrier((ga, gb, base, rms))
    ka, sa, kb, sb = added(added_kernel, "add2", ka, ga, kb, gb)
    ga, gb = swap(sa, Y, 3), swap(sb, X, 1)
    na, nb = renew(base, rms, ka, ga, kb, gb)

    na, nb = joined(False, na, swap(na, Y, 3), nb, swap(nb, X, 1))
    na, nb = joined(False, na, swap(na, Y, 1), nb, swap(nb, Y, 3))
    ga, gb = swap(na, X, 1), swap(nb, Y, 1)
    na, nb, rim, meta = lax.optimization_barrier((na, nb, rim, meta))
    lo = attention(0, meta, queries, (rim,), keys, values)
    ga, gb, lo = lax.optimization_barrier((ga, gb, lo))
    (mine,) = joined(True, na, ga, nb, gb)
    other = swap(mine, CORE, 1)
    mixed, squares = outputs(queries, lo, hi, mine, other)
    sums = ring_sum(squares)
    fresh = weights_out(me, mine, other)
    result = norm(mixed, *sums, head_gain, lax.axis_size(HEAD) * dim)
    return result, fresh


def solution(mesh):
    seqs = 2
    sizes = mesh.shape
    fine = Mesh(
        mesh.devices.reshape(sizes["ctx"] // 4, 2, 2, seqs, sizes["hs"] // seqs),
        (Y, X, CORE, SEQ, HEAD),
    )
    ctx, hs = (Y, X, CORE), (SEQ, HEAD)
    return jax.shard_map(
        per_device,
        mesh=fine,
        in_specs=(
            P(hs, ctx, None),
            P(hs, ctx, None),
            P(hs, ctx, None),
            P(hs, ctx),
            P(),
            P(hs, None, None, None),
            P(hs, None, None, None),
            P(hs, None),
        ),
        out_specs=(P(hs, ctx, None), P(hs, None, None, None)),
        check_vma=False,
    )
```

```python
import functools
import math

import jax
import jax.numpy as jnp
from jax import lax
from jax.experimental import pallas as pl
from jax.experimental.pallas import tpu as pltpu
from jax.sharding import Mesh, PartitionSpec as P

WINDOW = 512
TILE = 256
BLOCK = 32
MIB = 1024 * 1024
BF16 = jnp.bfloat16
F32 = jnp.float32
NEG = -1e30

Y, X, CORE, SEQ, HEAD = "y", "x", "core", "seq", "head"


def nt(a, b):
    return lax.dot_general(a, b, (((1,), (1,)), ((), ())), preferred_element_type=F32)


def nn(a, b):
    return lax.dot_general(a, b, (((1,), (0,)), ((), ())), preferred_element_type=F32)


def tn(a, b):
    return lax.dot_general(a, b, (((0,), (0,)), ((), ())), preferred_element_type=F32)


def whole():
    return pl.BlockSpec(memory_space=pltpu.VMEM)


def params(limit, **kw):
    return pltpu.CompilerParams(vmem_limit_bytes=limit * MIB, **kw)


def cost(flops, read, trans=0):
    return pl.CostEstimate(flops=int(flops), bytes_accessed=int(read), transcendentals=int(trans))


def column_of(row):
    return jnp.transpose(jnp.broadcast_to(row, (128, 128)))


def grad_kernel(inv, me_ref, k_ref, v_ref, r_ref, w_ref, keep_ref, send_ref, kk, uu, dd, acc):
    step = pl.program_id(0)
    last = pl.num_programs(0) - 1
    here = pl.ds(pl.multiple_of(step * TILE, TILE), TILE)
    keys = k_ref[0]
    kk[here, :] = keys
    tiles = TILE // 128
    parts = []
    for t in range(tiles):
        rate = column_of(r_ref[0:1, t * 128 : (t + 1) * 128])
        rows = v_ref[0, t * 128 : (t + 1) * 128, :].astype(F32)
        wide = jnp.concatenate([rate] * (rows.shape[1] // 128), axis=1)
        parts.append((wide * rows * inv).astype(BF16))
    u = jnp.concatenate(parts, axis=0)
    uu[here, :] = u
    h1 = nn(keys, w_ref[0, 0])
    h3 = nn(keys, w_ref[0, 1])
    dg = nn(u, w_ref[0, 2])
    sig = 0.5 + 0.5 * jnp.tanh(0.5 * h1)
    act = h1 * sig
    dd[0, here, :] = (dg * h3 * (sig + act * (1.0 - sig))).astype(BF16)
    dd[1, here, :] = (dg * act).astype(BF16)
    dd[2, here, :] = (act * h3).astype(BF16)

    @pl.when(step == last)
    def _():
        acc[0] = tn(dd[0], kk[...]).astype(BF16)
        acc[1] = tn(dd[1], kk[...]).astype(BF16)
        acc[2] = tn(dd[2], uu[...]).astype(BF16)
        chips = keep_ref.shape[0]
        core = me_ref[0] // chips
        for d in range(chips):
            for o, ref in ((core, keep_ref), (1 - core, send_ref)):
                at = pl.multiple_of((o * chips + d) * BLOCK, BLOCK)
                ref[d] = acc[:, pl.ds(at, BLOCK), :]


def gradients(me, keys, values, rates, weights, inv):
    rows, dim = keys.shape[1:]
    hidden = weights.shape[3]
    out = jax.ShapeDtypeStruct((hidden // BLOCK // 2, 3, BLOCK, dim), BF16)
    tile = pl.BlockSpec((1, TILE, dim), lambda i, s: (0, i, 0))
    return pl.pallas_call(
        functools.partial(grad_kernel, inv),
        grid_spec=pltpu.PrefetchScalarGridSpec(
            num_scalar_prefetch=1,
            grid=(rows // TILE,),
            in_specs=[
                tile,
                tile,
                pl.BlockSpec((1, TILE), lambda i, s: (0, i)),
                pl.BlockSpec(weights.shape, lambda i, s: (0, 0, 0, 0)),
            ],
            out_specs=[whole()] * 2,
            scratch_shapes=[
                pltpu.VMEM((rows, dim), BF16),
                pltpu.VMEM((rows, dim), BF16),
                pltpu.VMEM((3, rows, hidden), BF16),
                pltpu.VMEM((3, hidden, dim), BF16),
            ],
        ),
        out_shape=[out, out],
        compiler_params=params(24),
        cost_estimate=cost(1000, MIB),
        name="grad",
    )(me, keys, values, rates, weights)


def rim_kernel(k_ref, v_ref, rim_ref):
    rim_ref[0] = k_ref[0]
    rim_ref[1] = v_ref[0]


def rim_of(keys, values):
    rows, dim = keys.shape[1:]
    end = pl.BlockSpec((1, WINDOW, dim), lambda i: (0, rows // WINDOW - 1, 0))
    return pl.pallas_call(
        rim_kernel,
        grid=(1,),
        in_specs=[end, end],
        out_specs=whole(),
        out_shape=jax.ShapeDtypeStruct((2, WINDOW, dim), BF16),
        compiler_params=params(6),
        cost_estimate=cost(1, 3 * MIB),
        name="rim",
    )(keys, values)


def attend(q, ks, vs, first, low, scale):
    tile = q.shape[0]
    col = lax.broadcasted_iota(jnp.int32, (tile, tile), 1)
    row = lax.broadcasted_iota(jnp.int32, (tile, tile), 0)
    scores = []
    for b in range(3):
        s = nt(q, ks[b])
        ok = col >= low - (first + b * tile)
        if b == 2:
            ok = ok & (col <= row)
        scores.append(jnp.where(ok, s, NEG))
    top = jnp.max(jnp.maximum(jnp.maximum(scores[0], scores[1]), scores[2]), axis=1, keepdims=True)
    total, out = None, None
    for b in range(3):
        p = jnp.exp2((scores[b] - top) * scale)
        total = p if total is None else total + p
        o = nn(p.astype(BF16), vs[b])
        out = o if out is None else out + o
    return out / jnp.sum(total, axis=1, keepdims=True)


def lowest(meta_ref, first, tile):
    pos = first + 2 * tile + lax.broadcasted_iota(jnp.int32, (tile, 1), 0)
    low = jnp.zeros_like(pos)
    for b in range(1, 4):
        low = jnp.where(pos >= meta_ref[b], meta_ref[b], low)
    return jnp.maximum(low, pos - (WINDOW - 1))


def bounds_kernel(place_ref, docs_ref, meta_ref):
    docs = docs_ref[...]
    own = lax.broadcasted_iota(jnp.int32, docs.shape, 0) == place_ref[1]
    meta_ref[0] = place_ref[2]
    for b in range(1, 4):
        meta_ref[b] = jnp.sum(jnp.where(own & (docs < b), 1.0, 0.0)).astype(jnp.int32)


def bounds(place, docs):
    return pl.pallas_call(
        bounds_kernel,
        grid=(1,),
        in_specs=[pl.BlockSpec(memory_space=pltpu.SMEM), pl.BlockSpec(docs.shape, lambda i: (0, 0))],
        out_specs=pl.BlockSpec(memory_space=pltpu.SMEM),
        out_shape=jax.ShapeDtypeStruct((4,), jnp.int32),
        compiler_params=params(4),
        cost_estimate=cost(6 * docs.size, 4 * docs.size),
        name="bounds",
    )(place, docs)


def attn_kernel(scale, part, meta_ref, *refs):
    if part == 0:
        q_ref, rim_ref, k_ref, v_ref, o_ref = refs
    else:
        q_ref, k_ref, v_ref, o_ref = refs
    for t in range(WINDOW // TILE):
        first = meta_ref[0] + part * WINDOW + (t - 2) * TILE
        ks, vs = [], []
        for b in range(3):
            at = part * WINDOW + (t + b - 2) * TILE
            if at < 0:
                at += WINDOW
                ks.append(rim_ref[0, at : at + TILE, :])
                vs.append(rim_ref[1, at : at + TILE, :])
            else:
                ks.append(k_ref[0, at : at + TILE, :])
                vs.append(v_ref[0, at : at + TILE, :])
        q = q_ref[0, t * TILE : (t + 1) * TILE, :]
        o_ref[t * TILE : (t + 1) * TILE, :] = attend(
            q, ks, vs, first, lowest(meta_ref, first, TILE), scale
        )


def attention(part, meta, queries, rims, keys, values):
    dim = queries.shape[2]
    rows = keys.shape[1] if part else WINDOW
    smem = pl.BlockSpec(memory_space=pltpu.SMEM)
    own = pl.BlockSpec((1, rows, dim), lambda i: (0, 0, 0))
    rim = pl.BlockSpec((2, WINDOW, dim), lambda i: (0, 0, 0))
    return pl.pallas_call(
        functools.partial(attn_kernel, math.log2(math.e) / math.sqrt(dim), part),
        grid=(1,),
        in_specs=[smem, pl.BlockSpec((1, WINDOW, dim), lambda i: (0, part, 0))]
        + [rim] * len(rims)
        + [own, own],
        out_specs=pl.BlockSpec((WINDOW, dim), lambda i: (0, 0)),
        out_shape=jax.ShapeDtypeStruct((WINDOW, dim), F32),
        compiler_params=params(14),
        cost_estimate=cost(4 * WINDOW * 3 * TILE * dim, 4 * MIB, 3 * WINDOW * TILE),
        name="attn" + "ab"[part],
    )(meta, queries, *rims, keys, values)


def prep_kernel(me_ref, w_ref, m_ref, base_ref, rms_ref, wt, mt):
    at = pl.multiple_of(me_ref[0] % (128 // BLOCK) * BLOCK, BLOCK)
    for m in range(3):
        wt[...] = jnp.transpose(w_ref[0, m].astype(F32))
        mt[...] = jnp.transpose(m_ref[0, m])
        w = wt[pl.ds(at, BLOCK), :]
        base_ref[m] = w - 0.9 * mt[pl.ds(at, BLOCK), :]
        rms = jnp.sqrt(jnp.mean(w * w, axis=1, keepdims=True) + 1e-06)
        rms_ref[m] = jnp.broadcast_to(rms, (BLOCK, 128))


def prepare(me, weights, momentum):
    dim = weights.shape[2]
    pick = pl.BlockSpec((1, 3, dim, 128), lambda i, s: (0, 0, 0, s[0] // (128 // BLOCK)))
    shapes = [(3, BLOCK, dim), (3, BLOCK, 128)]
    return pl.pallas_call(
        prep_kernel,
        grid_spec=pltpu.PrefetchScalarGridSpec(
            num_scalar_prefetch=1,
            grid=(1,),
            in_specs=[pick] * 2,
            out_specs=[whole()] * 2,
            scratch_shapes=[pltpu.VMEM((128, dim), F32)] * 2,
        ),
        out_shape=[jax.ShapeDtypeStruct(shape, F32) for shape in shapes],
        compiler_params=params(8),
        cost_estimate=cost(3 * MIB, 3 * MIB),
        name="prep",
    )(me, weights, momentum)


def renew_kernel(base_ref, rms_ref, pieces_ref, out_ref):
    cand = base_ref[...]
    for d in range(pieces_ref.shape[0]):
        cand = cand + pieces_ref[d].astype(F32)
    new = lax.rsqrt(jnp.mean(cand * cand, axis=2, keepdims=True) + 1e-06)
    rows = (cand * (rms_ref[...][:, :, :1] * new)).astype(BF16)
    for d in range(out_ref.shape[0]):
        out_ref[d] = rows


def renew(base, rms, pieces):
    return pl.pallas_call(
        renew_kernel,
        in_specs=[whole()] * 3,
        out_specs=whole(),
        out_shape=jax.ShapeDtypeStruct(pieces.shape, BF16),
        compiler_params=params(8),
        cost_estimate=cost(MIB, MIB),
        name="renew",
    )(base, rms, pieces)


def fill(new, mine_ref, other_ref):
    chips, _, block, dim = mine_ref.shape
    size = chips * block
    for m in range(3):
        new[m, :size, :] = mine_ref[:, m].reshape(size, dim)
        new[m, size:, :] = other_ref[:, m].reshape(size, dim)


def out_kernel(q_ref, lo_ref, hi_ref, mine_ref, other_ref, y_ref, ss_ref, new):
    step = pl.program_id(0)

    @pl.when(step == 0)
    def _():
        fill(new, mine_ref, other_ref)

    q = q_ref[0]
    one = nt(q, new[0])
    three = nt(q, new[1])
    gq = (one * (0.5 + 0.5 * jnp.tanh(0.5 * one)) * three).astype(BF16)
    attn = jnp.where(step < pl.num_programs(0) // 2, lo_ref[...], hi_ref[...])
    y = attn + nn(gq, new[2])
    y_ref[...] = y
    sq = y * y
    lanes = sq[:, :128]
    for c in range(1, sq.shape[1] // 128):
        lanes = lanes + sq[:, c * 128 : (c + 1) * 128]
    tiles = TILE // 128
    for t in range(tiles):
        turned = jnp.transpose(lanes[t * 128 : (t + 1) * 128, :])
        row = jnp.sum(turned, axis=0, keepdims=True)
        for h in range(ss_ref.shape[0]):
            ss_ref[h, pl.ds(step * tiles + t, 1), :] = row


def outputs(queries, lo, hi, mine, other, copies):
    rows, dim = queries.shape[1:]
    hidden = 2 * mine.shape[0] * BLOCK
    mid = rows // TILE // 2
    tile = pl.BlockSpec((TILE, dim), lambda i: (i, 0))
    low = pl.BlockSpec((TILE, dim), lambda i: (jnp.minimum(i, mid - 1), 0))
    high = pl.BlockSpec((TILE, dim), lambda i: (jnp.maximum(i - mid, 0), 0))
    return pl.pallas_call(
        out_kernel,
        grid=(rows // TILE,),
        in_specs=[pl.BlockSpec((1, TILE, dim), lambda i: (0, i, 0)), low, high, whole(), whole()],
        out_specs=[tile, whole()],
        out_shape=[
            jax.ShapeDtypeStruct((rows, dim), F32),
            jax.ShapeDtypeStruct((copies, rows // 128, 128), F32),
        ],
        scratch_shapes=[pltpu.VMEM((3, hidden, dim), BF16)],
        compiler_params=params(14),
        cost_estimate=cost(6 * rows * dim * hidden, 6 * MIB, rows * hidden),
        name="out",
    )(queries, lo, hi, mine, other)


def final_kernel(count, me_ref, y_ref, sums_ref, gain_ref, mine_ref, other_ref, out_ref, new_ref, rows):
    step = pl.program_id(0)
    chips = mine_ref.shape[0]
    own = me_ref[0] // chips == step // 2
    for m in range(3):
        for b in range(chips // 2):
            at = step % 2 * (chips // 2) + b
            rows[m, b * BLOCK : (b + 1) * BLOCK, :] = jnp.where(
                own, mine_ref[at, m], other_ref[at, m]
            )
        new_ref[0, m] = jnp.transpose(rows[m])
    tiles = y_ref.shape[0] // 128
    dim = y_ref.shape[1]
    gain = gain_ref[...]
    for t in range(tiles):
        at = pl.ds(step * tiles + t, 1)
        total = sums_ref[0, at, :]
        for h in range(1, sums_ref.shape[0]):
            total = total + sums_ref[h, at, :]
        scale = column_of(lax.rsqrt(total * (1.0 / count) + 1e-06))
        wide = jnp.concatenate([scale] * (dim // 128), axis=1)
        part = slice(t * 128, (t + 1) * 128)
        out_ref[0, part, :] = (y_ref[part, :] * wide * gain).astype(BF16)


def final(me, y, sums, gain, mine, other, count):
    rows, dim = y.shape
    hidden = 2 * mine.shape[0] * BLOCK
    steps = 4
    full = lambda shape: pl.BlockSpec(shape, lambda i: (0,) * len(shape))
    return pl.pallas_call(
        functools.partial(final_kernel, count),
        grid=(steps,),
        in_specs=[
            pl.BlockSpec(memory_space=pltpu.SMEM),
            pl.BlockSpec((rows // steps, dim), lambda i: (i, 0)),
            full(sums.shape),
            full((1, dim)),
            whole(),
            whole(),
        ],
        out_specs=[
            pl.BlockSpec((1, rows // steps, dim), lambda i: (0, i, 0)),
            pl.BlockSpec((1, 3, dim, hidden // steps), lambda i: (0, 0, 0, i)),
        ],
        out_shape=[
            jax.ShapeDtypeStruct((1, rows, dim), BF16),
            jax.ShapeDtypeStruct((1, 3, dim, hidden), BF16),
        ],
        scratch_shapes=[pltpu.VMEM((3, hidden // steps, dim), BF16)],
        compiler_params=params(16),
        cost_estimate=cost(MIB, 6 * MIB),
        name="final",
    )(me, y, sums, gain, mine, other)


def swap(x, axis, by):
    return lax.ppermute(x, axis, [(i, i ^ by) for i in range(lax.axis_size(axis))])


def added_kernel(a_ref, b_ref, out_ref):
    out_ref[...] = (a_ref[...].astype(F32) + b_ref[...].astype(F32)).astype(BF16)


def added(a, b):
    return pl.pallas_call(
        added_kernel,
        in_specs=[whole()] * 2,
        out_specs=whole(),
        out_shape=jax.ShapeDtypeStruct(a.shape, BF16),
        compiler_params=params(8),
        cost_estimate=cost(MIB, MIB),
        name="added",
    )(a, b)


def per_device(queries, keys, values, rates, doc_ids, fast_weights, momentum, head_gain):
    rows, dim = queries.shape[1:]
    y, x, core = lax.axis_index(Y), lax.axis_index(X), lax.axis_index(CORE)
    ctx = (Y, X, CORE)
    n = lax.axis_size(Y) * lax.axis_size(X) * lax.axis_size(CORE)
    chip = y * lax.axis_size(X) + x
    me = core * (n // 2) + chip
    offset = lax.axis_index(ctx) * rows
    me = jnp.stack([me, lax.axis_index(SEQ), offset]).astype(jnp.int32)
    inv = 1.0 / math.sqrt(rows * n)
    hbm = lambda array: pltpu.with_memory_space_constraint(array, pltpu.HBM)

    rim = rim_of(hbm(keys), hbm(values))
    rim, me = lax.optimization_barrier((rim, me))
    rim = lax.ppermute(rim, ctx, [(i, (i + 1) % n) for i in range(n)])
    keep, send = gradients(me, hbm(keys), hbm(values), rates, hbm(fast_weights), inv)
    got = swap(send, CORE, 1)
    keep, me = lax.optimization_barrier((keep, me))
    base, rms = prepare(me, fast_weights, momentum)
    meta = bounds(me, doc_ids)
    hi = attention(1, meta, queries, (), keys, values)
    got, base, rms, rim, hi, meta = lax.optimization_barrier((got, base, rms, rim, hi, meta))
    pieces = lax.all_to_all(added(keep, got), (Y, X), 0, 0)

    mine = lax.all_to_all(renew(base, rms, pieces), (Y, X), 0, 0)
    other = swap(mine, CORE, 1)
    mine, rim, meta = lax.optimization_barrier((mine, rim, meta))
    lo = attention(0, meta, queries, (rim,), keys, values)
    other, lo = lax.optimization_barrier((other, lo))
    heads = lax.axis_size(HEAD)
    mixed, squares = outputs(queries, lo, hi, mine, other, heads)
    sums = lax.all_to_all(squares, HEAD, 0, 0)
    result, fresh = final(me, mixed, sums, head_gain, mine, other, heads * dim)
    return result, fresh


def solution(mesh):
    seqs = 2
    sizes = mesh.shape
    fine = Mesh(
        mesh.devices.reshape(sizes["ctx"] // 4, 2, 2, seqs, sizes["hs"] // seqs),
        (Y, X, CORE, SEQ, HEAD),
    )
    ctx, hs = (Y, X, CORE), (SEQ, HEAD)
    return jax.shard_map(
        per_device,
        mesh=fine,
        in_specs=(
            P(hs, ctx, None),
            P(hs, ctx, None),
            P(hs, ctx, None),
            P(hs, ctx),
            P(),
            P(hs, None, None, None),
            P(hs, None, None, None),
            P(hs, None),
        ),
        out_specs=(P(hs, ctx, None), P(hs, None, None, None)),
        check_vma=False,
    )
```

```python
import functools
import math

import jax
import jax.numpy as jnp
from jax import lax
from jax.experimental import pallas as pl
from jax.experimental.pallas import tpu as pltpu
from jax.sharding import Mesh, PartitionSpec as P

WINDOW = 512
TILE = 256
OUT_TILE = 512
BLOCK = 32
MIB = 1024 * 1024
BF16 = jnp.bfloat16
F32 = jnp.float32
NEG = -1e30

Y, X, CORE, SEQ, HEAD = "y", "x", "core", "seq", "head"


def nt(a, b):
    return lax.dot_general(a, b, (((1,), (1,)), ((), ())), preferred_element_type=F32)


def nn(a, b):
    return lax.dot_general(a, b, (((1,), (0,)), ((), ())), preferred_element_type=F32)


def tn(a, b):
    return lax.dot_general(a, b, (((0,), (0,)), ((), ())), preferred_element_type=F32)


def whole():
    return pl.BlockSpec(memory_space=pltpu.VMEM)


def params(limit, **kw):
    return pltpu.CompilerParams(vmem_limit_bytes=limit * MIB, **kw)


def cost(flops, read, trans=0):
    return pl.CostEstimate(flops=int(flops), bytes_accessed=int(read), transcendentals=int(trans))


def column_of(row):
    return jnp.transpose(jnp.broadcast_to(row, (128, 128)))


def load_kernel(part, k_ref, v_ref, out_ref, sems):
    rows = pl.ds(part * WINDOW, WINDOW)
    copies = [
        pltpu.make_async_copy(ref.at[0, rows, :], out_ref.at[j], sems.at[j])
        for j, ref in enumerate((k_ref, v_ref))
    ]
    for copy in copies:
        copy.start()
    for copy in copies:
        copy.wait()


def load(part, keys, values):
    return pl.pallas_call(
        functools.partial(load_kernel, part),
        in_specs=[pl.BlockSpec(memory_space=pl.ANY)] * 2,
        out_specs=whole(),
        out_shape=jax.ShapeDtypeStruct((2, WINDOW, keys.shape[2]), BF16),
        scratch_shapes=[pltpu.SemaphoreType.DMA((2,))],
        compiler_params=params(6),
        cost_estimate=cost(1, 2 * MIB),
        name="load" + "ab"[part],
    )(keys, values)


def grad_kernel(own, inv, me_ref, first_ref, last_ref, r_ref, w_ref, out_ref):
    chips, _, block, dim = out_ref.shape
    half = chips * block
    core = me_ref[0] // chips
    units = pl.ds(pl.multiple_of((core if own else 1 - core) * half, half), half)
    sums = [None] * 3
    for c, ref in enumerate((first_ref, last_ref)):
        keys = ref[0]
        parts = []
        for t in range(WINDOW // 128):
            at = c * WINDOW + t * 128
            rate = column_of(r_ref[0:1, at : at + 128] * inv)
            rows = ref[1, t * 128 : (t + 1) * 128, :].astype(F32)
            wide = jnp.concatenate([rate] * (dim // 128), axis=1)
            parts.append((wide * rows).astype(BF16))
        u = jnp.concatenate(parts, axis=0)
        h1 = nn(keys, w_ref[0, 0, :, units])
        h3 = nn(keys, w_ref[0, 1, :, units])
        dg = nn(u, w_ref[0, 2, :, units])
        sig = 0.5 + 0.5 * jnp.tanh(0.5 * h1)
        act = h1 * sig
        parts = (
            tn((dg * h3 * (sig + act * (1.0 - sig))).astype(BF16), keys),
            tn((dg * act).astype(BF16), keys),
            tn((act * h3).astype(BF16), u),
        )
        sums = [p if s is None else s + p for s, p in zip(sums, parts)]
    for m in range(3):
        out_ref[:, m] = sums[m].reshape(chips, block, dim).astype(BF16)


def gradients(own, me, first, last, rates, weights, inv):
    rows, dim = 2 * WINDOW, first.shape[2]
    hidden = weights.shape[3] // 2
    chips = hidden // BLOCK
    return pl.pallas_call(
        functools.partial(grad_kernel, own, inv),
        in_specs=[pl.BlockSpec(memory_space=pltpu.SMEM)] + [whole()] * 4,
        out_specs=whole(),
        out_shape=jax.ShapeDtypeStruct((chips, 3, BLOCK, dim), BF16),
        compiler_params=params(24),
        cost_estimate=cost(1000, MIB),
        name="grad" + ("own" if own else "other"),
    )(me, first, last, rates, weights)


def attend(q, ks, vs, first, low, scale):
    tile = q.shape[0]
    col = lax.broadcasted_iota(jnp.int32, (tile, tile), 1)
    row = lax.broadcasted_iota(jnp.int32, (tile, tile), 0)
    scores = []
    for b in range(3):
        s = nt(q, ks[b])
        ok = col >= low - (first + b * tile)
        if b == 2:
            ok = ok & (col <= row)
        scores.append(jnp.where(ok, s, NEG))
    top = jnp.max(jnp.maximum(jnp.maximum(scores[0], scores[1]), scores[2]), axis=1, keepdims=True)
    total, out = None, None
    for b in range(3):
        p = jnp.exp2((scores[b] - top) * scale)
        total = p if total is None else total + p
        o = nn(p.astype(BF16), vs[b])
        out = o if out is None else out + o
    return out / jnp.sum(total, axis=1, keepdims=True)


def lowest(meta_ref, first, tile):
    pos = first + 2 * tile + lax.broadcasted_iota(jnp.int32, (tile, 1), 0)
    low = jnp.zeros_like(pos)
    for b in range(1, 4):
        low = jnp.where(pos >= meta_ref[b], meta_ref[b], low)
    return jnp.maximum(low, pos - (WINDOW - 1))


def bounds_kernel(place_ref, docs_ref, meta_ref):
    docs = docs_ref[...]
    own = lax.broadcasted_iota(jnp.int32, docs.shape, 0) == place_ref[1]
    meta_ref[0] = place_ref[2]
    for b in range(1, 4):
        meta_ref[b] = jnp.sum(jnp.where(own & (docs < b), 1.0, 0.0)).astype(jnp.int32)


def bounds(place, docs):
    return pl.pallas_call(
        bounds_kernel,
        grid=(1,),
        in_specs=[pl.BlockSpec(memory_space=pltpu.SMEM), pl.BlockSpec(docs.shape, lambda i: (0, 0))],
        out_specs=pl.BlockSpec(memory_space=pltpu.SMEM),
        out_shape=jax.ShapeDtypeStruct((4,), jnp.int32),
        compiler_params=params(4),
        cost_estimate=cost(6 * docs.size, 4 * docs.size),
        name="bounds",
    )(place, docs)


def attn_kernel(scale, part, meta_ref, q_ref, before_ref, own_ref, o_ref):
    for t in range(WINDOW // TILE):
        first = meta_ref[0] + part * WINDOW + (t - 2) * TILE
        ks, vs = [], []
        for b in range(3):
            at = (t + b) * TILE
            ref, at = (before_ref, at) if at < WINDOW else (own_ref, at - WINDOW)
            ks.append(ref[0, at : at + TILE, :])
            vs.append(ref[1, at : at + TILE, :])
        at = part * WINDOW + t * TILE
        q = q_ref[0, at : at + TILE, :]
        o_ref[t * TILE : (t + 1) * TILE, :] = attend(
            q, ks, vs, first, lowest(meta_ref, first, TILE), scale
        )


def attention(part, meta, queries, before, own):
    dim = queries.shape[2]
    return pl.pallas_call(
        functools.partial(attn_kernel, math.log2(math.e) / math.sqrt(dim), part),
        in_specs=[pl.BlockSpec(memory_space=pltpu.SMEM)] + [whole()] * 3,
        out_specs=whole(),
        out_shape=jax.ShapeDtypeStruct((WINDOW, dim), F32),
        compiler_params=params(14),
        cost_estimate=cost(4 * WINDOW * 3 * TILE * dim, 4 * MIB, 3 * WINDOW * TILE),
        name="attn" + "ab"[part],
    )(meta, queries, before, own)


def prep_kernel(me_ref, w_ref, m_ref, base_ref, rms_ref, wt, mt):
    at = pl.multiple_of(me_ref[0] % (128 // BLOCK) * BLOCK, BLOCK)
    for m in range(3):
        wt[...] = jnp.transpose(w_ref[0, m].astype(F32))
        mt[...] = jnp.transpose(m_ref[0, m])
        w = wt[pl.ds(at, BLOCK), :]
        base_ref[m] = w - 0.9 * mt[pl.ds(at, BLOCK), :]
        rms = jnp.sqrt(jnp.mean(w * w, axis=1, keepdims=True) + 1e-06)
        rms_ref[m] = jnp.broadcast_to(rms, (BLOCK, 128))


def prepare(me, weights, momentum):
    dim = weights.shape[2]
    pick = pl.BlockSpec((1, 3, dim, 128), lambda i, s: (0, 0, 0, s[0] // (128 // BLOCK)))
    shapes = [(3, BLOCK, dim), (3, BLOCK, 128)]
    return pl.pallas_call(
        prep_kernel,
        grid_spec=pltpu.PrefetchScalarGridSpec(
            num_scalar_prefetch=1,
            grid=(1,),
            in_specs=[pick] * 2,
            out_specs=[whole()] * 2,
            scratch_shapes=[pltpu.VMEM((128, dim), F32)] * 2,
        ),
        out_shape=[jax.ShapeDtypeStruct(shape, F32) for shape in shapes],
        compiler_params=params(8),
        cost_estimate=cost(3 * MIB, 3 * MIB),
        name="prep",
    )(me, weights, momentum)


def renew_kernel(base_ref, rms_ref, pieces_ref, out_ref):
    cand = base_ref[...]
    for d in range(pieces_ref.shape[0]):
        cand = cand + pieces_ref[d].astype(F32)
    new = lax.rsqrt(jnp.mean(cand * cand, axis=2, keepdims=True) + 1e-06)
    rows = (cand * (rms_ref[...][:, :, :1] * new)).astype(BF16)
    for d in range(out_ref.shape[0]):
        out_ref[d] = rows


def renew(base, rms, pieces):
    return pl.pallas_call(
        renew_kernel,
        in_specs=[whole()] * 3,
        out_specs=whole(),
        out_shape=jax.ShapeDtypeStruct(pieces.shape, BF16),
        compiler_params=params(8),
        cost_estimate=cost(MIB, MIB),
        name="renew",
    )(base, rms, pieces)


def fill(new, mine_ref, other_ref):
    chips, _, block, dim = mine_ref.shape
    size = chips * block
    for m in range(3):
        new[m, :size, :] = mine_ref[:, m].reshape(size, dim)
        new[m, size:, :] = other_ref[:, m].reshape(size, dim)


def out_kernel(q_ref, lo_ref, hi_ref, mine_ref, other_ref, y_ref, ss_ref, new):
    step = pl.program_id(0)

    @pl.when(step == 0)
    def _():
        fill(new, mine_ref, other_ref)

    q = q_ref[0]
    one = nt(q, new[0])
    three = nt(q, new[1])
    gq = (one * (0.5 + 0.5 * jnp.tanh(0.5 * one)) * three).astype(BF16)
    attn = jnp.where(step < pl.num_programs(0) // 2, lo_ref[...], hi_ref[...])
    y = attn + nn(gq, new[2])
    y_ref[...] = y
    sq = y * y
    lanes = sq[:, :128]
    for c in range(1, sq.shape[1] // 128):
        lanes = lanes + sq[:, c * 128 : (c + 1) * 128]
    tiles = OUT_TILE // 128
    for t in range(tiles):
        turned = jnp.transpose(lanes[t * 128 : (t + 1) * 128, :])
        row = jnp.sum(turned, axis=0, keepdims=True)
        for h in range(ss_ref.shape[0]):
            ss_ref[h, pl.ds(step * tiles + t, 1), :] = row


def outputs(queries, lo, hi, mine, other, copies):
    rows, dim = queries.shape[1:]
    hidden = 2 * mine.shape[0] * BLOCK
    mid = rows // OUT_TILE // 2
    tile = pl.BlockSpec((OUT_TILE, dim), lambda i: (i, 0))
    low = pl.BlockSpec((OUT_TILE, dim), lambda i: (jnp.minimum(i, mid - 1), 0))
    high = pl.BlockSpec((OUT_TILE, dim), lambda i: (jnp.maximum(i - mid, 0), 0))
    return pl.pallas_call(
        out_kernel,
        grid=(rows // OUT_TILE,),
        in_specs=[pl.BlockSpec((1, OUT_TILE, dim), lambda i: (0, i, 0)), low, high, whole(), whole()],
        out_specs=[tile, whole()],
        out_shape=[
            jax.ShapeDtypeStruct((rows, dim), F32),
            jax.ShapeDtypeStruct((copies, rows // 128, 128), F32),
        ],
        scratch_shapes=[pltpu.VMEM((3, hidden, dim), BF16)],
        compiler_params=params(14),
        cost_estimate=cost(6 * rows * dim * hidden, 6 * MIB, rows * hidden),
        name="out",
    )(queries, lo, hi, mine, other)


def final_kernel(count, me_ref, y_ref, sums_ref, gain_ref, mine_ref, other_ref, out_ref, new_ref, rows):
    step = pl.program_id(0)
    chips = mine_ref.shape[0]
    own = me_ref[0] // chips == step // 2
    for m in range(3):
        for b in range(chips // 2):
            at = step % 2 * (chips // 2) + b
            rows[m, b * BLOCK : (b + 1) * BLOCK, :] = jnp.where(
                own, mine_ref[at, m], other_ref[at, m]
            )
        new_ref[0, m] = jnp.transpose(rows[m])
    tiles = y_ref.shape[0] // 128
    dim = y_ref.shape[1]
    gain = gain_ref[...]
    for t in range(tiles):
        at = pl.ds(step * tiles + t, 1)
        total = sums_ref[0, at, :]
        for h in range(1, sums_ref.shape[0]):
            total = total + sums_ref[h, at, :]
        scale = column_of(lax.rsqrt(total * (1.0 / count) + 1e-06))
        wide = jnp.concatenate([scale] * (dim // 128), axis=1)
        part = slice(t * 128, (t + 1) * 128)
        out_ref[0, part, :] = (y_ref[part, :] * wide * gain).astype(BF16)


def final(me, y, sums, gain, mine, other, count):
    rows, dim = y.shape
    hidden = 2 * mine.shape[0] * BLOCK
    steps = 4
    full = lambda shape: pl.BlockSpec(shape, lambda i: (0,) * len(shape))
    return pl.pallas_call(
        functools.partial(final_kernel, count),
        grid=(steps,),
        in_specs=[
            pl.BlockSpec(memory_space=pltpu.SMEM),
            pl.BlockSpec((rows // steps, dim), lambda i: (i, 0)),
            full(sums.shape),
            full((1, dim)),
            whole(),
            whole(),
        ],
        out_specs=[
            pl.BlockSpec((1, rows // steps, dim), lambda i: (0, i, 0)),
            pl.BlockSpec((1, 3, dim, hidden // steps), lambda i: (0, 0, 0, i)),
        ],
        out_shape=[
            jax.ShapeDtypeStruct((1, rows, dim), BF16),
            jax.ShapeDtypeStruct((1, 3, dim, hidden), BF16),
        ],
        scratch_shapes=[pltpu.VMEM((3, hidden // steps, dim), BF16)],
        compiler_params=params(16),
        cost_estimate=cost(MIB, 6 * MIB),
        name="final",
    )(me, y, sums, gain, mine, other)


def swap(x, axis, by):
    return lax.ppermute(x, axis, [(i, i ^ by) for i in range(lax.axis_size(axis))])


def added_kernel(a_ref, b_ref, out_ref):
    out_ref[...] = (a_ref[...].astype(F32) + b_ref[...].astype(F32)).astype(BF16)


def added(a, b):
    return pl.pallas_call(
        added_kernel,
        in_specs=[whole()] * 2,
        out_specs=whole(),
        out_shape=jax.ShapeDtypeStruct(a.shape, BF16),
        compiler_params=params(8),
        cost_estimate=cost(MIB, MIB),
        name="added",
    )(a, b)


def per_device(queries, keys, values, rates, doc_ids, fast_weights, momentum, head_gain):
    rows, dim = queries.shape[1:]
    y, x, core = lax.axis_index(Y), lax.axis_index(X), lax.axis_index(CORE)
    ctx = (Y, X, CORE)
    n = lax.axis_size(Y) * lax.axis_size(X) * lax.axis_size(CORE)
    chip = y * lax.axis_size(X) + x
    me = core * (n // 2) + chip
    offset = lax.axis_index(ctx) * rows
    me = jnp.stack([me, lax.axis_index(SEQ), offset]).astype(jnp.int32)
    inv = 1.0 / math.sqrt(rows * n)
    hbm = lambda array: pltpu.with_memory_space_constraint(array, pltpu.HBM)

    last = load(1, hbm(keys), hbm(values))
    last, me, weights = lax.optimization_barrier((last, me, fast_weights))
    rim = lax.ppermute(last, ctx, [(i, (i + 1) % n) for i in range(n)])
    keys, values, me = lax.optimization_barrier((keys, values, me, last))[:3]
    first = load(0, hbm(keys), hbm(values))
    send = gradients(False, me, first, last, rates, weights, inv)
    got = swap(send, CORE, 1)
    me, first = lax.optimization_barrier((me, first, send))[:2]
    keep = gradients(True, me, first, last, rates, weights, inv)
    keep, me = lax.optimization_barrier((keep, me))
    base, rms = prepare(me, weights, momentum)
    meta = bounds(me, doc_ids)
    hi = attention(1, meta, queries, first, last)
    got, base, rms, rim, hi, meta = lax.optimization_barrier((got, base, rms, rim, hi, meta))
    pieces = lax.all_to_all(added(keep, got), (Y, X), 0, 0)

    mine = lax.all_to_all(renew(base, rms, pieces), (Y, X), 0, 0)
    other = swap(mine, CORE, 1)
    mine, rim, meta = lax.optimization_barrier((mine, rim, meta))
    lo = attention(0, meta, queries, rim, first)
    other, lo = lax.optimization_barrier((other, lo))
    heads = lax.axis_size(HEAD)
    mixed, squares = outputs(queries, lo, hi, mine, other, heads)
    sums = lax.all_to_all(squares, HEAD, 0, 0)
    result, fresh = final(me, mixed, sums, head_gain, mine, other, heads * dim)
    return result, fresh


def solution(mesh):
    seqs = 2
    sizes = mesh.shape
    fine = Mesh(
        mesh.devices.reshape(sizes["ctx"] // 4, 2, 2, seqs, sizes["hs"] // seqs),
        (Y, X, CORE, SEQ, HEAD),
    )
    ctx, hs = (Y, X, CORE), (SEQ, HEAD)
    return jax.shard_map(
        per_device,
        mesh=fine,
        in_specs=(
            P(hs, ctx, None),
            P(hs, ctx, None),
            P(hs, ctx, None),
            P(hs, ctx),
            P(),
            P(hs, None, None, None),
            P(hs, None, None, None),
            P(hs, None),
        ),
        out_specs=(P(hs, ctx, None), P(hs, None, None, None)),
        check_vma=False,
    )
```

```python
import functools
import math

import jax
import jax.numpy as jnp
from jax import lax
from jax.experimental import pallas as pl
from jax.experimental.pallas import tpu as pltpu
from jax.sharding import Mesh, PartitionSpec as P

WINDOW = 512
TILE = 256
OUT_TILE = 512
BLOCK = 32
MIB = 1024 * 1024
BF16 = jnp.bfloat16
F32 = jnp.float32
NEG = -1e30

Y, X, CORE, SEQ, HEAD = "y", "x", "core", "seq", "head"


def nt(a, b):
    return lax.dot_general(a, b, (((1,), (1,)), ((), ())), preferred_element_type=F32)


def nn(a, b):
    return lax.dot_general(a, b, (((1,), (0,)), ((), ())), preferred_element_type=F32)


def tn(a, b):
    return lax.dot_general(a, b, (((0,), (0,)), ((), ())), preferred_element_type=F32)


def whole():
    return pl.BlockSpec(memory_space=pltpu.VMEM)


def params(limit, **kw):
    return pltpu.CompilerParams(vmem_limit_bytes=limit * MIB, **kw)


def cost(flops, read, trans=0):
    return pl.CostEstimate(flops=int(flops), bytes_accessed=int(read), transcendentals=int(trans))


def column_of(row):
    return jnp.transpose(jnp.broadcast_to(row, (128, 128)))


def load_kernel(part, k_ref, v_ref, out_ref, sems):
    rows = pl.ds(part * WINDOW, WINDOW)
    copies = [
        pltpu.make_async_copy(ref.at[0, rows, :], out_ref.at[j], sems.at[j])
        for j, ref in enumerate((k_ref, v_ref))
    ]
    for copy in copies:
        copy.start()
    for copy in copies:
        copy.wait()


def load(part, keys, values):
    return pl.pallas_call(
        functools.partial(load_kernel, part),
        in_specs=[pl.BlockSpec(memory_space=pl.ANY)] * 2,
        out_specs=whole(),
        out_shape=jax.ShapeDtypeStruct((2, WINDOW, keys.shape[2]), BF16),
        scratch_shapes=[pltpu.SemaphoreType.DMA((2,))],
        compiler_params=params(6),
        cost_estimate=cost(1, 2 * MIB),
        name="load" + "ab"[part],
    )(keys, values)


def grad_kernel(own, inv, me_ref, first_ref, last_ref, r_ref, w_ref, out_ref):
    chips, _, block, dim = out_ref.shape
    half = chips * block
    core = me_ref[0] // chips
    units = pl.ds(pl.multiple_of((core if own else 1 - core) * half, half), half)
    sums = [None] * 3
    for c, ref in enumerate((first_ref, last_ref)):
        keys = ref[0]
        parts = []
        for t in range(WINDOW // 128):
            at = c * WINDOW + t * 128
            rate = column_of(r_ref[0:1, at : at + 128] * inv)
            rows = ref[1, t * 128 : (t + 1) * 128, :].astype(F32)
            wide = jnp.concatenate([rate] * (dim // 128), axis=1)
            parts.append((wide * rows).astype(BF16))
        u = jnp.concatenate(parts, axis=0)
        h1 = nn(keys, w_ref[0, 0, :, units])
        h3 = nn(keys, w_ref[0, 1, :, units])
        dg = nn(u, w_ref[0, 2, :, units])
        sig = 0.5 + 0.5 * jnp.tanh(0.5 * h1)
        act = h1 * sig
        parts = (
            tn((dg * h3 * (sig + act * (1.0 - sig))).astype(BF16), keys),
            tn((dg * act).astype(BF16), keys),
            tn((act * h3).astype(BF16), u),
        )
        sums = [p if s is None else s + p for s, p in zip(sums, parts)]
    for m in range(3):
        out_ref[:, m] = sums[m].reshape(chips, block, dim).astype(BF16)


def gradients(own, me, first, last, rates, weights, inv):
    rows, dim = 2 * WINDOW, first.shape[2]
    hidden = weights.shape[3] // 2
    chips = hidden // BLOCK
    return pl.pallas_call(
        functools.partial(grad_kernel, own, inv),
        in_specs=[pl.BlockSpec(memory_space=pltpu.SMEM)] + [whole()] * 4,
        out_specs=whole(),
        out_shape=jax.ShapeDtypeStruct((chips, 3, BLOCK, dim), BF16),
        compiler_params=params(24),
        cost_estimate=cost(1000, MIB),
        name="grad" + ("own" if own else "other"),
    )(me, first, last, rates, weights)


def attend(q, ks, vs, first, low, scale):
    tile = q.shape[0]
    col = lax.broadcasted_iota(jnp.int32, (tile, tile), 1)
    row = lax.broadcasted_iota(jnp.int32, (tile, tile), 0)
    scores = []
    for b in range(3):
        s = nt(q, ks[b])
        ok = col >= low - (first + b * tile)
        if b == 2:
            ok = ok & (col <= row)
        scores.append(jnp.where(ok, s, NEG))
    top = jnp.max(jnp.maximum(jnp.maximum(scores[0], scores[1]), scores[2]), axis=1, keepdims=True)
    total, out = None, None
    for b in range(3):
        p = jnp.exp2((scores[b] - top) * scale)
        total = p if total is None else total + p
        o = nn(p.astype(BF16), vs[b])
        out = o if out is None else out + o
    return out / jnp.sum(total, axis=1, keepdims=True)


def lowest(meta_ref, first, tile):
    pos = first + 2 * tile + lax.broadcasted_iota(jnp.int32, (tile, 1), 0)
    low = jnp.zeros_like(pos)
    for b in range(1, 4):
        low = jnp.where(pos >= meta_ref[b], meta_ref[b], low)
    return jnp.maximum(low, pos - (WINDOW - 1))


def bounds_kernel(place_ref, docs_ref, meta_ref):
    docs = docs_ref[...]
    own = lax.broadcasted_iota(jnp.int32, docs.shape, 0) == place_ref[1]
    meta_ref[0] = place_ref[2]
    for b in range(1, 4):
        meta_ref[b] = jnp.sum(jnp.where(own & (docs < b), 1.0, 0.0)).astype(jnp.int32)


def bounds(place, docs):
    return pl.pallas_call(
        bounds_kernel,
        grid=(1,),
        in_specs=[pl.BlockSpec(memory_space=pltpu.SMEM), pl.BlockSpec(docs.shape, lambda i: (0, 0))],
        out_specs=pl.BlockSpec(memory_space=pltpu.SMEM),
        out_shape=jax.ShapeDtypeStruct((4,), jnp.int32),
        compiler_params=params(4),
        cost_estimate=cost(6 * docs.size, 4 * docs.size),
        name="bounds",
    )(place, docs)


def attn_kernel(scale, part, meta_ref, q_ref, before_ref, own_ref, o_ref):
    for t in range(WINDOW // TILE):
        first = meta_ref[0] + part * WINDOW + (t - 2) * TILE
        ks, vs = [], []
        for b in range(3):
            at = (t + b) * TILE
            ref, at = (before_ref, at) if at < WINDOW else (own_ref, at - WINDOW)
            ks.append(ref[0, at : at + TILE, :])
            vs.append(ref[1, at : at + TILE, :])
        at = part * WINDOW + t * TILE
        q = q_ref[0, at : at + TILE, :]
        o_ref[t * TILE : (t + 1) * TILE, :] = attend(
            q, ks, vs, first, lowest(meta_ref, first, TILE), scale
        )


def attention(part, meta, queries, before, own):
    dim = queries.shape[2]
    return pl.pallas_call(
        functools.partial(attn_kernel, math.log2(math.e) / math.sqrt(dim), part),
        in_specs=[pl.BlockSpec(memory_space=pltpu.SMEM)] + [whole()] * 3,
        out_specs=whole(),
        out_shape=jax.ShapeDtypeStruct((WINDOW, dim), F32),
        compiler_params=params(14),
        cost_estimate=cost(4 * WINDOW * 3 * TILE * dim, 4 * MIB, 3 * WINDOW * TILE),
        name="attn" + "ab"[part],
    )(meta, queries, before, own)


def prep_kernel(me_ref, w_ref, m_ref, base_ref, rms_ref, wt, mt):
    at = pl.multiple_of(me_ref[0] % (128 // BLOCK) * BLOCK, BLOCK)
    for m in range(3):
        wt[...] = jnp.transpose(w_ref[0, m].astype(F32))
        mt[...] = jnp.transpose(m_ref[0, m])
        w = wt[pl.ds(at, BLOCK), :]
        base_ref[m] = w - 0.9 * mt[pl.ds(at, BLOCK), :]
        rms = jnp.sqrt(jnp.mean(w * w, axis=1, keepdims=True) + 1e-06)
        rms_ref[m] = jnp.broadcast_to(rms, (BLOCK, 128))


def prepare(me, weights, momentum):
    dim = weights.shape[2]
    pick = pl.BlockSpec((1, 3, dim, 128), lambda i, s: (0, 0, 0, s[0] // (128 // BLOCK)))
    shapes = [(3, BLOCK, dim), (3, BLOCK, 128)]
    return pl.pallas_call(
        prep_kernel,
        grid_spec=pltpu.PrefetchScalarGridSpec(
            num_scalar_prefetch=1,
            grid=(1,),
            in_specs=[pick] * 2,
            out_specs=[whole()] * 2,
            scratch_shapes=[pltpu.VMEM((128, dim), F32)] * 2,
        ),
        out_shape=[jax.ShapeDtypeStruct(shape, F32) for shape in shapes],
        compiler_params=params(8),
        cost_estimate=cost(3 * MIB, 3 * MIB),
        name="prep",
    )(me, weights, momentum)


def renew_kernel(base_ref, rms_ref, pieces_ref, out_ref):
    cand = base_ref[...]
    for d in range(pieces_ref.shape[0]):
        cand = cand + pieces_ref[d].astype(F32)
    new = lax.rsqrt(jnp.mean(cand * cand, axis=2, keepdims=True) + 1e-06)
    rows = (cand * (rms_ref[...][:, :, :1] * new)).astype(BF16)
    for d in range(out_ref.shape[0]):
        out_ref[d] = rows


def renew(base, rms, pieces):
    return pl.pallas_call(
        renew_kernel,
        in_specs=[whole()] * 3,
        out_specs=whole(),
        out_shape=jax.ShapeDtypeStruct(pieces.shape, BF16),
        compiler_params=params(8),
        cost_estimate=cost(MIB, MIB),
        name="renew",
    )(base, rms, pieces)


def fill(new, mine_ref, other_ref):
    chips, _, block, dim = mine_ref.shape
    size = chips * block
    for m in range(3):
        new[m, :size, :] = mine_ref[:, m].reshape(size, dim)
        new[m, size:, :] = other_ref[:, m].reshape(size, dim)


def out_kernel(q_ref, lo_ref, hi_ref, mine_ref, other_ref, y_ref, ss_ref, new):
    step = pl.program_id(0)

    @pl.when(step == 0)
    def _():
        fill(new, mine_ref, other_ref)

    q = q_ref[0]
    one = nt(q, new[0])
    three = nt(q, new[1])
    gq = (one * (0.5 + 0.5 * jnp.tanh(0.5 * one)) * three).astype(BF16)
    attn = jnp.where(step < pl.num_programs(0) // 2, lo_ref[...], hi_ref[...])
    y = attn + nn(gq, new[2])
    y_ref[...] = y
    sq = y * y
    lanes = sq[:, :128]
    for c in range(1, sq.shape[1] // 128):
        lanes = lanes + sq[:, c * 128 : (c + 1) * 128]
    tiles = OUT_TILE // 128
    for t in range(tiles):
        turned = jnp.transpose(lanes[t * 128 : (t + 1) * 128, :])
        row = jnp.sum(turned, axis=0, keepdims=True)
        for h in range(ss_ref.shape[0]):
            ss_ref[h, pl.ds(step * tiles + t, 1), :] = row


def outputs(queries, lo, hi, mine, other, copies):
    rows, dim = queries.shape[1:]
    hidden = 2 * mine.shape[0] * BLOCK
    mid = rows // OUT_TILE // 2
    tile = pl.BlockSpec((OUT_TILE, dim), lambda i: (i, 0))
    low = pl.BlockSpec((OUT_TILE, dim), lambda i: (jnp.minimum(i, mid - 1), 0))
    high = pl.BlockSpec((OUT_TILE, dim), lambda i: (jnp.maximum(i - mid, 0), 0))
    return pl.pallas_call(
        out_kernel,
        grid=(rows // OUT_TILE,),
        in_specs=[pl.BlockSpec((1, OUT_TILE, dim), lambda i: (0, i, 0)), low, high, whole(), whole()],
        out_specs=[tile, whole()],
        out_shape=[
            jax.ShapeDtypeStruct((rows, dim), F32),
            jax.ShapeDtypeStruct((copies, rows // 128, 128), F32),
        ],
        scratch_shapes=[pltpu.VMEM((3, hidden, dim), BF16)],
        compiler_params=params(14),
        cost_estimate=cost(6 * rows * dim * hidden, 6 * MIB, rows * hidden),
        name="out",
    )(queries, lo, hi, mine, other)


def final_kernel(count, me_ref, y_ref, sums_ref, gain_ref, mine_ref, other_ref, out_ref, new_ref, rows):
    step = pl.program_id(0)
    chips = mine_ref.shape[0]
    own = me_ref[0] // chips == step
    for m in range(3):
        for b in range(chips):
            rows[m, b * BLOCK : (b + 1) * BLOCK, :] = jnp.where(
                own, mine_ref[b, m], other_ref[b, m]
            )
        new_ref[0, m] = jnp.transpose(rows[m])
    tiles = y_ref.shape[0] // 128
    dim = y_ref.shape[1]
    gain = gain_ref[...]
    for t in range(tiles):
        at = pl.ds(step * tiles + t, 1)
        total = sums_ref[0, at, :]
        for h in range(1, sums_ref.shape[0]):
            total = total + sums_ref[h, at, :]
        scale = column_of(lax.rsqrt(total * (1.0 / count) + 1e-06))
        wide = jnp.concatenate([scale] * (dim // 128), axis=1)
        part = slice(t * 128, (t + 1) * 128)
        out_ref[0, part, :] = (y_ref[part, :] * wide * gain).astype(BF16)


def final(me, y, sums, gain, mine, other, count):
    rows, dim = y.shape
    hidden = 2 * mine.shape[0] * BLOCK
    steps = 2
    full = lambda shape: pl.BlockSpec(shape, lambda i: (0,) * len(shape))
    return pl.pallas_call(
        functools.partial(final_kernel, count),
        grid=(steps,),
        in_specs=[
            pl.BlockSpec(memory_space=pltpu.SMEM),
            pl.BlockSpec((rows // steps, dim), lambda i: (i, 0)),
            full(sums.shape),
            full((1, dim)),
            whole(),
            whole(),
        ],
        out_specs=[
            pl.BlockSpec((1, rows // steps, dim), lambda i: (0, i, 0)),
            pl.BlockSpec((1, 3, dim, hidden // steps), lambda i: (0, 0, 0, i)),
        ],
        out_shape=[
            jax.ShapeDtypeStruct((1, rows, dim), BF16),
            jax.ShapeDtypeStruct((1, 3, dim, hidden), BF16),
        ],
        scratch_shapes=[pltpu.VMEM((3, hidden // steps, dim), BF16)],
        compiler_params=params(16),
        cost_estimate=cost(MIB, 6 * MIB),
        name="final",
    )(me, y, sums, gain, mine, other)


def swap(x, axis, by):
    return lax.ppermute(x, axis, [(i, i ^ by) for i in range(lax.axis_size(axis))])


def added_kernel(a_ref, b_ref, out_ref):
    out_ref[...] = (a_ref[...].astype(F32) + b_ref[...].astype(F32)).astype(BF16)


def added(a, b):
    return pl.pallas_call(
        added_kernel,
        in_specs=[whole()] * 2,
        out_specs=whole(),
        out_shape=jax.ShapeDtypeStruct(a.shape, BF16),
        compiler_params=params(8),
        cost_estimate=cost(MIB, MIB),
        name="added",
    )(a, b)


def per_device(queries, keys, values, rates, doc_ids, fast_weights, momentum, head_gain):
    rows, dim = queries.shape[1:]
    y, x, core = lax.axis_index(Y), lax.axis_index(X), lax.axis_index(CORE)
    ctx = (Y, X, CORE)
    n = lax.axis_size(Y) * lax.axis_size(X) * lax.axis_size(CORE)
    chip = y * lax.axis_size(X) + x
    me = core * (n // 2) + chip
    offset = lax.axis_index(ctx) * rows
    me = jnp.stack([me, lax.axis_index(SEQ), offset]).astype(jnp.int32)
    inv = 1.0 / math.sqrt(rows * n)
    hbm = lambda array: pltpu.with_memory_space_constraint(array, pltpu.HBM)

    last = load(1, hbm(keys), hbm(values))
    last, me, weights = lax.optimization_barrier((last, me, fast_weights))
    rim = lax.ppermute(last, ctx, [(i, (i + 1) % n) for i in range(n)])
    keys, values, me = lax.optimization_barrier((keys, values, me, last))[:3]
    first = load(0, hbm(keys), hbm(values))
    send = gradients(False, me, first, last, rates, weights, inv)
    got = swap(send, CORE, 1)
    me, first = lax.optimization_barrier((me, first, send))[:2]
    keep = gradients(True, me, first, last, rates, weights, inv)
    keep, me = lax.optimization_barrier((keep, me))
    base, rms = prepare(me, weights, momentum)
    meta = bounds(me, doc_ids)
    hi = attention(1, meta, queries, first, last)
    got, base, rms, rim, hi, meta = lax.optimization_barrier((got, base, rms, rim, hi, meta))
    pieces = lax.all_to_all(added(keep, got), (Y, X), 0, 0)

    mine = lax.all_to_all(renew(base, rms, pieces), (Y, X), 0, 0)
    other = swap(mine, CORE, 1)
    mine, rim, meta = lax.optimization_barrier((mine, rim, meta))
    lo = attention(0, meta, queries, rim, first)
    other, lo = lax.optimization_barrier((other, lo))
    heads = lax.axis_size(HEAD)
    mixed, squares = outputs(queries, lo, hi, mine, other, heads)
    sums = lax.all_to_all(squares, HEAD, 0, 0)
    result, fresh = final(me, mixed, sums, head_gain, mine, other, heads * dim)
    return result, fresh


def solution(mesh):
    seqs = 2
    sizes = mesh.shape
    fine = Mesh(
        mesh.devices.reshape(sizes["ctx"] // 4, 2, 2, seqs, sizes["hs"] // seqs),
        (Y, X, CORE, SEQ, HEAD),
    )
    ctx, hs = (Y, X, CORE), (SEQ, HEAD)
    return jax.shard_map(
        per_device,
        mesh=fine,
        in_specs=(
            P(hs, ctx, None),
            P(hs, ctx, None),
            P(hs, ctx, None),
            P(hs, ctx),
            P(),
            P(hs, None, None, None),
            P(hs, None, None, None),
            P(hs, None),
        ),
        out_specs=(P(hs, ctx, None), P(hs, None, None, None)),
        check_vma=False,
    )
```
